32 devices in a mesh: grp: 2 (over x), gz: 8 (over z, y), ba: 2 (over core).
Axes of the slice: x: 2, y: 2, z: 4, core: 2. Of those that a mesh axis runs over, the one named last changes fastest.
Arguments:
- cosmology: bfloat16 [512, 8], P(('grp', 'gz', 'ba')), parts along dimension 0, may hold values from -4 to 4
- trunk_in: bfloat16 [8, 512], replicated, may hold values from -2 to 2
- trunk_mid: bfloat16 [512, 512], replicated, may hold values from -0.25 to 0.25
- trunk_out: bfloat16 [512, 256], replicated, may hold values from -0.25 to 0.25
- head_weight: bfloat16 [16, 256, 2048], P('gz'), may hold values from -0.375 to 0.375
- band_width: int32 [16, 100], P('gz'), may hold values from 1 to 64, 2048 in all within a row
- band_weight: float32 [16, 2048], P('gz'), may hold values from 0.25 to 4
- kernels: float32 [10, 16], replicated, may hold values from 0.2 to 1
- pair_bins: int32 [55, 2], replicated, may hold values from 0 to 9
- target: float32 [512, 55, 100], P(('grp', 'gz', 'ba')), parts along dimension 0, may hold values from -6 to 6
- head_moment: float32 [16, 256, 2048], P('gz', None, 'ba'), may hold values from -6 to 6
- head_square: float32 [16, 256, 2048], P('gz', None, 'ba'), may hold values from 0.5 to 4
- in_moment: float32 [8, 512], P(None, ('gz', 'ba')), may hold values from -6 to 6
- in_square: float32 [8, 512], P(None, ('gz', 'ba')), may hold values from 0.5 to 4
- mid_moment: float32 [512, 512], P(None, ('gz', 'ba')), may hold values from -6 to 6
- mid_square: float32 [512, 512], P(None, ('gz', 'ba')), may hold values from 0.003 to 315
- out_moment: float32 [512, 256], P(None, ('gz', 'ba')), may hold values from -6 to 6
- out_square: float32 [512, 256], P(None, ('gz', 'ba')), may hold values from 0.003 to 315
Outputs:
- spectra: float32 [512, 55, 100], P(('grp', 'gz', 'ba')), parts along dimension 0
- head_new: bfloat16 [16, 512, 2048], P('gz', 'grp', 'ba'), parts along dimension 1
- head_moment_new: float32 [16, 512, 2048], P('gz', 'grp', 'ba'), parts along dimension 1
- head_square_new: float32 [16, 512, 2048], P('gz', 'grp', 'ba'), parts along dimension 1
- in_new: bfloat16 [16, 512], P('grp', ('gz', 'ba')), parts along dimension 0
- in_moment_new: float32 [16, 512], P('grp', ('gz', 'ba')), parts along dimension 0
- in_square_new: float32 [16, 512], P('grp', ('gz', 'ba')), parts along dimension 0
- mid_new: bfloat16 [1024, 512], P('grp', ('gz', 'ba')), parts along dimension 0
- mid_moment_new: float32 [1024, 512], P('grp', ('gz', 'ba')), parts along dimension 0
- mid_square_new: float32 [1024, 512], P('grp', ('gz', 'ba')), parts along dimension 0
- out_new: bfloat16 [1024, 256], P('grp', ('gz', 'ba')), parts along dimension 0
- out_moment_new: float32 [1024, 256], P('grp', ('gz', 'ba')), parts along dimension 0
- out_square_new: float32 [1024, 256], P('grp', ('gz', 'ba')), parts along dimension 0
The draws below stay inside these ranges and needn't reach their ends.
There are 2 independent parts, one for each index of `grp`. The reference program is written for one: setup_inputs(seed, part) draws one part's arguments, and reference() takes and returns one part's arrays. A program takes and returns all parts, laid end to end along the dimension named above; an argument that names none is the same for every part. Nothing has to cross between parts.
Inputs may be any that keep to these rules, and one draw needn't show every extreme that they name: `band_width`: each row of 100 band widths sums to 2048, and its widest band has 64 cells.
All inputs are finite; a program needn't handle non-finite values.
Results may differ from the reference program's by a relative error of at most 0.02.
Values may be sent and summed in bfloat16 or wider, within the bound.
A program may use at most 128 MiB of HBM per device.

```python
import math
import jax
import jax.numpy as jnp
import numpy as np
from jax import lax

NK = 2048
NELL = 100
NBIN = 10
NPAIR = 55
NPAR = 8
TW = 512
H = 256
BANDMAX = 64
NZ = 16
BATCH = 256


def entry_spread(key, row_count, column_count):
    logs = jax.random.uniform(key, (row_count, column_count), jnp.float32, -4.6, 4.6)
    return jnp.exp(logs)


def draw_mid_square(key, part):
    return entry_spread(jax.random.fold_in(key, 501), TW, TW)


def draw_out_square(key, part):
    return entry_spread(jax.random.fold_in(key, 733), TW, H)


def plant(drawn, stream_key, least, largest):
    place = [jax.random.randint(jax.random.fold_in(stream_key, axis), (), 0, length) for axis, length in enumerate(drawn.shape)]
    widest = drawn.shape.index(max(drawn.shape))
    neighbour = place[:widest] + [(place[widest] + 1) % drawn.shape[widest]] + place[widest + 1:]
    return drawn.at[tuple(place)].set(least).at[tuple(neighbour)].set(largest)


def levels(stream_key, extent, shards, least, largest):
    gain, own = 1.0, jax.random.fold_in(stream_key, 6)
    for position, shards_of in shards:
        steps = jnp.exp(jax.random.uniform(jax.random.fold_in(own, position), (shards_of,), jnp.float32, least / len(shards), largest / len(shards)))
        gain = gain * jnp.repeat(steps, extent[position] // shards_of).reshape([-1 if axis == position else 1 for axis in range(len(extent))])
    return gain


def profile(amount, total, limit, skew):
    portions = [(1 << 20) // math.isqrt(standing ** skew) + 1 for standing in range(2, amount + 1)]
    rest, counts = total - limit - (amount - 1), [1] * (amount - 1)
    while rest > 0:
        candidates = [i for i in range(amount - 1) if counts[i] < limit]
        mass, budget = sum([portions[i] for i in candidates]), rest
        for i in candidates:
            addition = min(limit - counts[i], max(1, budget * portions[i] // mass), rest)
            counts[i] = counts[i] + addition
            rest = rest - addition
    return np.array([limit] + counts)


def ragged_sizes(stream_key, count, total, limit, slope):
    if count == 2:
        one = jax.random.randint(stream_key, (), max(1, total - limit), min(limit, total - 1) + 1)
        return jnp.stack([one, total - one])
    lengths = jnp.asarray(profile(count, total, limit, slope), jnp.int32)
    couples = (count - 1) // 2
    giver, receiver = lengths[1:1 + 2 * couples:2], lengths[2:2 + 2 * couples:2]
    slack = jnp.minimum(giver - 1, limit - receiver)
    passed = jax.random.randint(jax.random.fold_in(stream_key, 1), (couples,), 0, 1 << 20) % (slack + 1)
    lengths = lengths.at[1:1 + 2 * couples:2].set(giver - passed).at[2:2 + 2 * couples:2].set(receiver + passed)
    return lengths[jax.random.permutation(jax.random.fold_in(stream_key, 2), count)]


def centred(own_key, extent, deviation, reach, split=(), kind=jnp.bfloat16):
    level = levels(own_key, extent, split, -0.22, 0.18) if split else 1.0
    array = jax.random.normal(own_key, extent, jnp.float32) * deviation * level
    return jnp.minimum(jnp.maximum(array, -reach), reach).astype(kind)


def setup_inputs(seed: int = 0, part: int = 0) -> dict:
    streams_of = jax.random.split(jax.random.key(seed), 19)
    part_splits = jax.random.split(jax.random.fold_in(streams_of[18], part), 19)
    return {
        "cosmology": centred(part_splits[0], (BATCH, NPAR), 1.0, 4.0, ((0, 16),)),
        "trunk_in": centred(streams_of[1], (NPAR, TW), NPAR ** -0.5, 2.0),
        "trunk_mid": centred(streams_of[2], (TW, TW), TW ** -0.5, 0.25),
        "trunk_out": centred(streams_of[3], (TW, H), TW ** -0.5, 0.25),
        "head_weight": centred(streams_of[4], (NZ, H, NK), H ** -0.5, 0.375, ((0, 8),)),
        "band_width": jax.vmap(lambda own: ragged_sizes(own, NELL, NK, BANDMAX, 2))(jax.random.split(streams_of[5], NZ)).reshape((NZ, NELL)).astype(jnp.int32),
        "band_weight": jnp.clip(jnp.exp(math.log(4.0) - 2.7725887 * jax.random.uniform(streams_of[6], (NZ, NK), jnp.float32) ** levels(streams_of[6], (NZ, NK), ((0, 8),), -0.2, 0.2)), 0.25, 4.0),
        "kernels": jnp.clip(jax.random.uniform(streams_of[7], (NBIN, NZ), jnp.float32, 0.2, 1.0), 0.2, 1.0),
        "pair_bins": plant(jax.random.randint(streams_of[8], (NPAIR, 2), 0, NBIN), jax.random.fold_in(streams_of[8], 1), 0, NBIN - 1).astype(jnp.int32),
        "target": centred(part_splits[9], (BATCH, NPAIR, NELL), 1.0, 6.0, ((0, 16),), jnp.float32),
        "head_moment": centred(streams_of[10], (NZ, H, NK), 1.0, 6.0, ((0, 8), (2, 2)), jnp.float32),
        "head_square": jnp.clip(jnp.exp(math.log(4.0) - 2.0794415 * jax.random.uniform(streams_of[11], (NZ, H, NK), jnp.float32) ** levels(streams_of[11], (NZ, H, NK), ((0, 8), (2, 2)), -0.2, 0.2)), 0.5, 4.0),
        "in_moment": centred(streams_of[12], (NPAR, TW), 1.0, 6.0, ((1, 16),), jnp.float32),
        "in_square": jnp.clip(jnp.exp(math.log(4.0) - 2.0794415 * jax.random.uniform(streams_of[13], (NPAR, TW), jnp.float32) ** levels(streams_of[13], (NPAR, TW), ((1, 16),), -0.2, 0.2)), 0.5, 4.0),
        "mid_moment": centred(streams_of[14], (TW, TW), 1.0, 6.0, ((1, 16),), jnp.float32),
        "mid_square": draw_mid_square(jax.random.fold_in(streams_of[18], 71), part),
        "out_moment": centred(streams_of[16], (TW, H), 1.0, 6.0, ((1, 16),), jnp.float32),
        "out_square": draw_out_square(jax.random.fold_in(streams_of[18], 71), part),
    }


learn_rate = 0.001
beta_first = 0.9
beta_second = 0.999
adam_epsilon = 1e-08

def silu_slope(values):
    sigmoid = jax.nn.sigmoid(values)
    return sigmoid * (1.0 + values * (1.0 - sigmoid))

def adam_step(weight, moment, square, gradient):
    moment_new = beta_first * moment + (1.0 - beta_first) * gradient
    square_new = beta_second * square + (1.0 - beta_second) * gradient * gradient
    updated = weight.astype(moment.dtype) - learn_rate * moment_new / (jnp.sqrt(square_new) + adam_epsilon)
    return (updated.astype(jnp.bfloat16), moment_new, square_new)

def band_matrix(widths, weights):
    ends = jnp.cumsum(widths, axis=-1).astype(jnp.int32)
    starts = ends - widths
    cells = jnp.arange(weights.shape[-1], dtype=jnp.int32)
    member = (starts[..., :, None] <= cells) & (cells < ends[..., :, None])
    weighted = jnp.where(member, weights[..., None, :], 0.0)
    return (weighted / lax.optimization_barrier(jnp.sum(weighted, axis=-1, keepdims=True))).astype(jnp.bfloat16)

def reference(cosmology, trunk_in, trunk_mid, trunk_out, head_weight, band_width, band_weight, kernels, pair_bins, target, head_moment, head_square, in_moment, in_square, mid_moment, mid_square, out_moment, out_square):
    highest = lax.Precision.HIGHEST
    pre_in = jnp.dot(cosmology, trunk_in, preferred_element_type=jnp.float32)
    act_in = jax.nn.silu(pre_in).astype(jnp.bfloat16)
    pre_mid = jnp.dot(act_in, trunk_mid, preferred_element_type=jnp.float32)
    act_mid = jax.nn.silu(pre_mid).astype(jnp.bfloat16)
    pre_out = jnp.dot(act_mid, trunk_out, preferred_element_type=jnp.float32)
    hidden = jax.nn.silu(pre_out).astype(jnp.bfloat16)
    pair_weight = kernels[pair_bins[:, 0]] * kernels[pair_bins[:, 1]] * (8.0 / math.sqrt(NZ))

    def forward_slice(total, sliced):
        weight_slice, width_slice, cell_weight, pair_slice = sliced
        projection = band_matrix(width_slice, cell_weight)
        power = jnp.dot(hidden, weight_slice, preferred_element_type=jnp.float32).astype(jnp.bfloat16)
        band_power = jnp.dot(power, projection.T, preferred_element_type=jnp.float32)
        return (total + pair_slice[None, :, None] * band_power[:, None, :], projection)
    start_total = jnp.zeros((BATCH, NPAIR, NELL), jnp.float32)
    spectra, projections = lax.scan(forward_slice, start_total, (head_weight, band_width, band_weight, pair_weight.T))
    residual = spectra - target

    def backward_slice(total, sliced):
        weight_slice, projection, pair_slice = sliced
        band_cot = jnp.einsum('bpl,p->bl', residual, pair_slice, precision=highest).astype(jnp.bfloat16)
        power_cot = jnp.dot(band_cot, projection, preferred_element_type=jnp.float32).astype(jnp.bfloat16)
        gradient = jnp.dot(power_cot.T, hidden, preferred_element_type=jnp.float32).T
        return (total + jnp.dot(power_cot, weight_slice.T, preferred_element_type=jnp.float32), gradient)
    start_cot = jnp.zeros((BATCH, H), jnp.float32)
    hidden_cot, head_grad = lax.scan(backward_slice, start_cot, (head_weight, projections, pair_weight.T))
    out_cot = (hidden_cot * silu_slope(pre_out)).astype(jnp.bfloat16)
    out_grad = jnp.dot(act_mid.T, out_cot, preferred_element_type=jnp.float32)
    mid_cot = (jnp.dot(out_cot, trunk_out.T, preferred_element_type=jnp.float32) * silu_slope(pre_mid)).astype(jnp.bfloat16)
    mid_grad = jnp.dot(act_in.T, mid_cot, preferred_element_type=jnp.float32)
    in_cot = (jnp.dot(mid_cot, trunk_mid.T, preferred_element_type=jnp.float32) * silu_slope(pre_in)).astype(jnp.bfloat16)
    in_grad = jnp.dot(cosmology.T, in_cot, preferred_element_type=jnp.float32)
    head_new, head_moment_new, head_square_new = adam_step(head_weight, head_moment, head_square, head_grad)
    in_new, in_moment_new, in_square_new = adam_step(trunk_in, in_moment, in_square, in_grad)
    mid_new, mid_moment_new, mid_square_new = adam_step(trunk_mid, mid_moment, mid_square, mid_grad)
    out_new, out_moment_new, out_square_new = adam_step(trunk_out, out_moment, out_square, out_grad)
    return (spectra, head_new, head_moment_new, head_square_new, in_new, in_moment_new, in_square_new, mid_new, mid_moment_new, mid_square_new, out_new, out_moment_new, out_square_new)
```

```python
import functools
import math

import jax
import jax.numpy as jnp
from jax import lax
from jax.experimental import pallas as pl
from jax.experimental.pallas import tpu as pltpu
from jax.sharding import PartitionSpec as P

learn_rate = 0.001
beta_first = 0.9
beta_second = 0.999
adam_epsilon = 1e-08
lanes = 128
MESH = pl.DeviceIdType.MESH
highest = lax.Precision.HIGHEST


def adam_step(weight, moment, square, gradient):
    moment_new = beta_first * moment + (1.0 - beta_first) * gradient
    square_new = beta_second * square + (1.0 - beta_second) * gradient * gradient
    updated = weight.astype(jnp.float32) - learn_rate * moment_new / (
        jnp.sqrt(square_new) + adam_epsilon
    )
    return (updated.astype(jnp.bfloat16), moment_new, square_new)


def nn(a, b, precision=None):
    return lax.dot_general(
        a, b, (((1,), (0,)), ((), ())), preferred_element_type=jnp.float32, precision=precision
    )


def nt(a, b, precision=None):
    return lax.dot_general(
        a, b, (((1,), (1,)), ((), ())), preferred_element_type=jnp.float32, precision=precision
    )


def tn(a, b, precision=None):
    return lax.dot_general(
        a, b, (((0,), (0,)), ((), ())), preferred_element_type=jnp.float32, precision=precision
    )


def split(values):
    high = values.astype(jnp.bfloat16)
    low = (values - high.astype(jnp.float32)).astype(jnp.bfloat16)
    return high, low


def iota(shape, axis):
    return lax.broadcasted_iota(jnp.int32, shape, axis)


def onehot(shape, offset, dtype=jnp.bfloat16):
    return (iota(shape, 0) + offset == iota(shape, 1)).astype(dtype)


def quotient(values, by):
    if by & (by - 1) == 0:
        return values >> (by.bit_length() - 1)
    return values // by


def remainder(values, by):
    if by & (by - 1) == 0:
        return values & (by - 1)
    return values % by


def step_kernel(slabs, halves, total_slices, *refs):
    inputs, refs = refs[:18], refs[18:]
    made, held, refs = refs[:13], refs[13:31], refs[31:]
    spectra_out, head_out, mid_out, out_out, in_out = (
        made[0],
        made[1:4],
        made[4:7],
        made[7:10],
        made[10:13],
    )
    (
        cos_t,
        trunk_in,
        trunk_mid,
        trunk_out,
        head_weight,
        band_width,
        band_weight,
        kernels,
        pair_bins,
        target,
        head_moment,
        head_square,
        in_moment,
        in_square,
        mid_moment,
        mid_square,
        out_moment,
        out_square,
    ) = held
    (
        cos_all,
        act_in,
        act_mid,
        hidden,
        pre_mid,
        pre_out,
        projection,
        fold_high,
        fold_low,
        mix_high,
        mix_low,
        back_high,
        back_low,
        padded,
        bp_send,
        bp_recv,
        bc_send,
        bc_recv,
        hc_send,
        hc_recv,
        oc_all,
        outer,
        load_sem,
        send_1,
        recv_1,
        send_2,
        recv_2,
        send_3,
        recv_3,
        send_4,
        recv_4,
        send_5,
        recv_5,
    ) = refs
    group = lax.axis_index("grp")
    slab = lax.axis_index("gz")
    half = lax.axis_index("ba")
    count = slabs * halves
    me = slab * halves + half
    params, rows = cos_t.shape
    pairs, _, bands = target.shape
    slices, features, cells = head_weight.shape
    width = trunk_mid.shape[0]
    rows_half = slabs * rows
    rows_all = halves * rows_half

    loads = [
        pltpu.make_async_copy(source, kept, load_sem.at[i])
        for i, (source, kept) in enumerate(zip(inputs, held))
    ]
    order = (0, 5, 6, 4, 1, 2, 3, 7, 8, 9, 10, 11, 12, 13, 14, 15, 16, 17)
    for i in order:
        loads[i].start()

    def place(index):
        return (group, quotient(index, halves), remainder(index, halves))

    def turn(first, last, body):
        if last - first <= 16:
            for d in range(first, last):
                body(d)
        else:

            def step(d, carry):
                body(d)
                return carry

            lax.fori_loop(first, last, step, 0)

    def all_peers(body):
        turn(1, count, lambda d: body(remainder(me + d, count)))

    def slab_peers(body):
        turn(1, slabs, lambda d: body(remainder(slab + d, slabs)))

    barrier = pltpu.get_barrier_semaphore()
    all_peers(
        lambda i: pl.semaphore_signal(barrier, inc=1, device_id=place(i), device_id_type=MESH)
    )
    loads[0].wait()
    cos_own = nt(onehot((rows, rows), 0), cos_t[...]).astype(jnp.bfloat16)
    cos_all[half, slab] = cos_own
    pl.semaphore_wait(barrier, count - 1)

    def copy_1(target_index, slot):
        return pltpu.make_async_remote_copy(
            src_ref=cos_all.at[half, slab],
            dst_ref=cos_all.at[remainder(slot, halves), quotient(slot, halves)],
            send_sem=send_1.at[target_index],
            recv_sem=recv_1.at[slot],
            device_id=place(target_index),
            device_id_type=MESH,
        )

    all_peers(lambda i: copy_1(i, me).start())

    loads[5].wait()
    loads[6].wait()
    triangle = iota((lanes, bands), 0)
    column = iota((lanes, bands), 1)
    widths = band_width[...].astype(jnp.float32).astype(jnp.bfloat16)
    ends = nt((triangle >= column).astype(jnp.bfloat16), widths).astype(jnp.int32)
    starts = nt((triangle > column).astype(jnp.bfloat16), widths).astype(jnp.int32)
    cell = iota((lanes, cells), 1)
    for s in range(slices):
        member = (starts[:, s : s + 1] <= cell) & (cell < ends[:, s : s + 1])
        weighted = jnp.where(member, band_weight[s : s + 1, :], 0.0)
        total = jnp.maximum(jnp.sum(weighted, axis=1, keepdims=True), 1e-30)
        projection[s] = (weighted * (1.0 / total)).astype(jnp.bfloat16)
    loads[4].wait()
    for s in range(slices):
        high, low = split(nt(projection[s], head_weight[s]))
        fold_high[s] = high
        fold_low[s] = low

    for i in (1, 2, 3):
        loads[i].wait()

    def forward(part):
        cosmology = cos_all[part].reshape(rows_half, params)
        pre = nn(cosmology, trunk_in[...])
        act = (pre * jax.nn.sigmoid(pre)).astype(jnp.bfloat16)
        act_in[part] = act
        pre = nn(act, trunk_mid[...])
        pre_mid[part] = pre
        act = (pre * jax.nn.sigmoid(pre)).astype(jnp.bfloat16)
        act_mid[part] = act
        pre = nn(act, trunk_out[...])
        pre_out[part] = pre.reshape(slabs, rows, features)
        act = (pre * jax.nn.sigmoid(pre)).astype(jnp.bfloat16)
        hidden[part] = act
        return act

    def slope(values):
        sigmoid = jax.nn.sigmoid(values)
        return sigmoid * (1.0 + values * (1.0 - sigmoid))

    def other_halves(body):
        for shift in range(1, halves):
            body(lax.rem(half + shift, halves))

    slab_peers(lambda j: copy_1(me, j * halves + half).wait_recv())
    features_half = forward(half)
    for s in range(slices):
        power = nt(features_half, fold_high[s]) + nt(features_half, fold_low[s])
        bp_send[:, s] = power.astype(jnp.bfloat16).reshape(slabs, rows, lanes)

    def copy_2(j, slot):
        return pltpu.make_async_remote_copy(
            src_ref=bp_send.at[j],
            dst_ref=bp_recv.at[slot],
            send_sem=send_2.at[j],
            recv_sem=recv_2.at[slot],
            device_id=(group, j, half),
            device_id_type=MESH,
        )

    slab_peers(lambda j: copy_2(j, slab).start())
    bp_recv[slab] = bp_send[slab]

    for i in (7, 8, 9):
        loads[i].wait()
    mixed = total_slices * rows
    spread = padded.shape[0] * rows
    bins = kernels.shape[0]
    weights = 8.0 / math.sqrt(total_slices)
    for side in range(2):
        chosen = (iota((bins, pairs), 0) == pair_bins[side : side + 1, :]).astype(jnp.float32)
        weights = weights * tn(kernels[...], chosen, highest)
    pair_lane = (
        quotient(iota((pairs, spread), 1), rows) == iota((pairs, spread), 0)
    ).astype(jnp.bfloat16)
    pair_row = (
        quotient(iota((spread, pairs), 0), rows) == iota((spread, pairs), 1)
    ).astype(jnp.bfloat16)
    slice_row = (
        quotient(iota((mixed, total_slices), 0), rows) == iota((mixed, total_slices), 1)
    ).astype(jnp.bfloat16)
    slice_lane = (
        quotient(iota((total_slices, mixed), 1), rows) == iota((total_slices, mixed), 0)
    ).astype(jnp.bfloat16)
    shape = (mixed, spread)
    same_back = remainder(iota(shape, 0), rows) == remainder(iota(shape, 1), rows)
    shape = (spread, mixed)
    same_mix = remainder(iota(shape, 0), rows) == remainder(iota(shape, 1), rows)
    for piece, mix, back in zip(
        split(weights), (mix_high, mix_low), (back_high, back_low)
    ):
        wide = nn(slice_row, nn(piece, pair_lane).astype(jnp.bfloat16))
        back[...] = jnp.where(same_back, wide, 0.0).astype(jnp.bfloat16)
        wide = nn(nt(pair_row, piece).astype(jnp.bfloat16), slice_lane)
        mix[...] = jnp.where(same_mix, wide, 0.0).astype(jnp.bfloat16)
    padded[...] = jnp.zeros_like(padded)

    slab_peers(lambda j: copy_2(slab, j).wait_recv())
    power = bp_recv[...].reshape(mixed, lanes)
    spectra = nn(mix_high[...], power) + nn(mix_low[...], power)
    spectra = spectra.reshape(padded.shape)[:pairs, :, :bands]
    spectra_out[...] = spectra
    padded[:pairs, :, :bands] = spectra - target[...]
    high, low = split(padded[...].reshape(spread, lanes))
    cot = nn(back_high[...], high) + nn(back_high[...], low) + nn(back_low[...], high)
    bc_send[...] = cot.astype(jnp.bfloat16).reshape(bc_send.shape)

    def copy_3(target_index, slot):
        return pltpu.make_async_remote_copy(
            src_ref=bc_send.at[quotient(target_index, halves)],
            dst_ref=bc_recv.at[remainder(slot, halves), quotient(slot, halves)],
            send_sem=send_3.at[target_index],
            recv_sem=recv_3.at[slot],
            device_id=place(target_index),
            device_id_type=MESH,
        )

    slab_peers(lambda j: copy_3(j * halves + half, me).start())

    def other_send(part):
        def start(j, carry):
            copy_3(j * halves + part, me).start()
            return carry

        lax.fori_loop(0, slabs, start, 0)

    other_halves(other_send)
    bc_recv[half, slab] = bc_send[slab]

    def other_forward(part):
        def wait(j, carry):
            copy_1(me, j * halves + part).wait_recv()
            return carry

        lax.fori_loop(0, slabs, wait, 0)
        forward(part)

    other_halves(other_forward)

    slab_peers(lambda j: copy_3(me, j * halves + half).wait_recv())
    cots = bc_recv[half]
    part = nn(cots[:, 0].reshape(rows_half, lanes), fold_high[0])
    for s in range(1, slices):
        part = part + nn(cots[:, s].reshape(rows_half, lanes), fold_high[s])
    hc_send[...] = part.astype(jnp.bfloat16).reshape(hc_send.shape)

    def copy_4(j, slot):
        return pltpu.make_async_remote_copy(
            src_ref=hc_send.at[j],
            dst_ref=hc_recv.at[slot],
            send_sem=send_4.at[j],
            recv_sem=recv_4.at[slot],
            device_id=(group, j, half),
            device_id_type=MESH,
        )

    slab_peers(lambda j: copy_4(j, slab).start())
    hc_recv[slab] = hc_send[slab]

    def other_cots(part):
        def wait(j, carry):
            copy_3(me, j * halves + part).wait_recv()
            return carry

        lax.fori_loop(0, slabs, wait, 0)

    other_halves(other_cots)
    hidden_all = hidden[...].reshape(rows_all, features)
    for s in range(slices):
        cots = bc_recv[:, :, s].reshape(rows_all, lanes)
        outer[s] = tn(hidden_all, cots).astype(jnp.bfloat16)
    for i in range(10, 18):
        loads[i].wait()
    half_cells = head_moment.shape[2]
    start = pl.multiple_of(half * half_cells, half_cells)
    own_cells = pl.ds(start, half_cells)
    block = 64

    def update_head(s):
        def step(i, carry):
            chunk = pl.ds(pl.multiple_of(i * block, block), block)
            gradient = nn(outer[s, chunk, :], projection[s, :, own_cells])
            new, moment, square = adam_step(
                head_weight[s, chunk, own_cells],
                head_moment[s, chunk, :],
                head_square[s, chunk, :],
                gradient,
            )
            head_out[0][s, chunk, :] = new
            head_out[1][s, chunk, :] = moment
            head_out[2][s, chunk, :] = square
            return carry

        lax.fori_loop(0, features // block, step, 0)

    for s in range(slices // 2):
        update_head(s)

    slab_peers(lambda j: copy_4(slab, j).wait_recv())
    cot = jnp.sum(hc_recv[...].astype(jnp.float32), axis=0)
    oc_all[half, slab] = (cot * slope(pre_out[half, slab])).astype(jnp.bfloat16)

    def copy_5(target_index, slot):
        return pltpu.make_async_remote_copy(
            src_ref=oc_all.at[half, slab],
            dst_ref=oc_all.at[remainder(slot, halves), quotient(slot, halves)],
            send_sem=send_5.at[target_index],
            recv_sem=recv_5.at[slot],
            device_id=place(target_index),
            device_id_type=MESH,
        )

    all_peers(lambda i: copy_5(i, me).start())
    mid_columns = mid_moment.shape[0]
    out_columns = out_moment.shape[0]
    pick_mid = onehot((mid_columns, width), me * mid_columns)
    pick_out = onehot((out_columns, features), me * out_columns)
    mid_own = nt(pick_mid, trunk_mid[...])
    out_own = nt(pick_out, trunk_out[...])
    in_own = nt(trunk_in[...], pick_mid)
    mid_rows = nn(pick_mid, trunk_mid[...]).astype(jnp.bfloat16)
    in_columns = nt(pick_mid, trunk_in[...]).astype(jnp.bfloat16)
    cosmology = cos_all[...].reshape(rows_all, params)
    in_slope = slope(nt(in_columns, cosmology))
    cosmology_t = nt(onehot((params, params), 0), cosmology).astype(jnp.bfloat16)
    for s in range(slices // 2, slices):
        update_head(s)
    mid_slope = slope(pre_mid[...].reshape(rows_all, width))
    all_peers(lambda i: copy_5(me, i).wait_recv())
    out_cot = oc_all[...].reshape(rows_all, features)
    mid_cot = (nt(out_cot, trunk_out[...]) * mid_slope).astype(jnp.bfloat16)
    out_cot_own = nt(pick_out, out_cot).astype(jnp.bfloat16)
    out_grad = nn(out_cot_own, act_mid[...].reshape(rows_all, width))
    mid_cot_own = nt(pick_mid, mid_cot).astype(jnp.bfloat16)
    mid_grad = nn(mid_cot_own, act_in[...].reshape(rows_all, width))
    in_cot_own = (nt(mid_rows, mid_cot) * in_slope).astype(jnp.bfloat16)
    in_grad = nt(cosmology_t, in_cot_own)
    for outs, own, moment, square, gradient in (
        (mid_out, mid_own, mid_moment, mid_square, mid_grad),
        (out_out, out_own, out_moment, out_square, out_grad),
        (in_out, in_own, in_moment, in_square, in_grad),
    ):
        updated = adam_step(own, moment[...], square[...], gradient)
        for out, value in zip(outs, updated):
            out[...] = value
    all_peers(lambda i: copy_1(i, me).wait_send())
    slab_peers(lambda j: copy_2(j, slab).wait_send())
    all_peers(lambda i: copy_3(i, me).wait_send())
    slab_peers(lambda j: copy_4(j, slab).wait_send())
    all_peers(lambda i: copy_5(i, me).wait_send())


def store_kernel(amount, *refs):
    sources, results, semaphores = refs[:amount], refs[amount : 2 * amount], refs[-1]
    stores = [
        pltpu.make_async_copy(source, result, semaphores.at[i])
        for i, (source, result) in enumerate(zip(sources, results))
    ]
    for store in stores:
        store.start()
    for store in stores:
        store.wait()


def shards(
    cosmology,
    trunk_in,
    trunk_mid,
    trunk_out,
    head_weight,
    band_width,
    band_weight,
    kernels,
    pair_bins,
    target,
    head_moment,
    head_square,
    in_moment,
    in_square,
    mid_moment,
    mid_square,
    out_moment,
    out_square,
):
    slabs = lax.axis_size("gz")
    halves = lax.axis_size("ba")
    count = slabs * halves
    rows, params = cosmology.shape
    pairs, bands = target.shape[1:]
    slices, features, cells = head_weight.shape
    width = trunk_mid.shape[0]
    rows_half = slabs * rows
    total_slices = slices * slabs
    mixed = total_slices * rows
    pairs_padded = pairs
    while pairs_padded * rows % lanes:
        pairs_padded += 1
    spread = pairs_padded * rows
    half_cells = cells // halves
    mid_columns = width // count
    out_columns = features // count
    bf16, f32 = jnp.bfloat16, jnp.float32
    hbm = pl.BlockSpec(memory_space=pltpu.HBM)
    vmem = pl.BlockSpec(memory_space=pltpu.VMEM)
    dma = pltpu.SemaphoreType.DMA
    inputs = (
        cosmology.T,
        trunk_in,
        trunk_mid,
        trunk_out,
        head_weight,
        band_width,
        band_weight,
        kernels,
        pair_bins.T,
        target.transpose(1, 0, 2),
        head_moment,
        head_square,
        in_moment,
        in_square,
        mid_moment.T,
        mid_square.T,
        out_moment.T,
        out_square.T,
    )
    inputs = tuple(pltpu.with_memory_space_constraint(a, pltpu.HBM) for a in inputs)
    out_shapes = [jax.ShapeDtypeStruct((pairs, rows, bands), f32)] + [
        jax.ShapeDtypeStruct(shape, dtype)
        for shape in (
            (slices, features, half_cells),
            (mid_columns, width),
            (out_columns, width),
            (params, mid_columns),
        )
        for dtype in (bf16, f32, f32)
    ]
    outs = pl.pallas_call(
        functools.partial(step_kernel, slabs, halves, total_slices),
        out_shape=[pltpu.VMEM(a.shape, a.dtype) for a in out_shapes],
        in_specs=[hbm] * len(inputs),
        out_specs=[vmem] * len(out_shapes),
        scratch_shapes=[pltpu.VMEM(a.shape, a.dtype) for a in inputs]
        + [
            pltpu.VMEM((halves, slabs, rows, params), bf16),
            pltpu.VMEM((halves, rows_half, width), bf16),
            pltpu.VMEM((halves, rows_half, width), bf16),
            pltpu.VMEM((halves, rows_half, features), bf16),
            pltpu.VMEM((halves, rows_half, width), f32),
            pltpu.VMEM((halves, slabs, rows, features), f32),
            pltpu.VMEM((slices, lanes, cells), bf16),
            pltpu.VMEM((slices, lanes, features), bf16),
            pltpu.VMEM((slices, lanes, features), bf16),
            pltpu.VMEM((spread, mixed), bf16),
            pltpu.VMEM((spread, mixed), bf16),
            pltpu.VMEM((mixed, spread), bf16),
            pltpu.VMEM((mixed, spread), bf16),
            pltpu.VMEM((pairs_padded, rows, lanes), f32),
            pltpu.VMEM((slabs, slices, rows, lanes), bf16),
            pltpu.VMEM((slabs, slices, rows, lanes), bf16),
            pltpu.VMEM((slabs, slices, rows, lanes), bf16),
            pltpu.VMEM((halves, slabs, slices, rows, lanes), bf16),
            pltpu.VMEM((slabs, rows, features), bf16),
            pltpu.VMEM((slabs, rows, features), bf16),
            pltpu.VMEM((halves, slabs, rows, features), bf16),
            pltpu.VMEM((slices, features, lanes), bf16),
            dma((len(inputs),)),
            dma((count,)),
            dma((count,)),
            dma((slabs,)),
            dma((slabs,)),
            dma((count,)),
            dma((count,)),
            dma((slabs,)),
            dma((slabs,)),
            dma((count,)),
            dma((count,)),
        ],
        compiler_params=pltpu.CompilerParams(
            collective_id=0, has_side_effects=True, vmem_limit_bytes=40 << 20
        ),
        name="step",
    )(*inputs)
    outs = pl.pallas_call(
        functools.partial(store_kernel, len(out_shapes)),
        out_shape=out_shapes,
        in_specs=[vmem] * len(out_shapes),
        out_specs=[hbm] * len(out_shapes),
        scratch_shapes=[dma((len(out_shapes),))],
        compiler_params=pltpu.CompilerParams(vmem_limit_bytes=16 << 20),
        name="store",
    )(*outs)
    spectra, head, mid, out, inner = outs[0], outs[1:4], outs[4:7], outs[7:10], outs[10:13]
    return (
        spectra.transpose(1, 0, 2),
        *head,
        *inner,
        *(a.T for a in mid),
        *(a.T for a in out),
    )


def solution(mesh):
    placed = (
        P(("grp", "gz", "ba"), None),
        P(),
        P(),
        P(),
        P("gz", None, None),
        P("gz", None),
        P("gz", None),
        P(),
        P(),
        P(("grp", "gz", "ba"), None, None),
        P("gz", None, "ba"),
        P("gz", None, "ba"),
        P(None, ("gz", "ba")),
        P(None, ("gz", "ba")),
        P(None, ("gz", "ba")),
        P(None, ("gz", "ba")),
        P(None, ("gz", "ba")),
        P(None, ("gz", "ba")),
    )
    return jax.shard_map(
        shards,
        mesh=mesh,
        in_specs=placed,
        out_specs=(
            P(("grp", "gz", "ba"), None, None),
            P("gz", "grp", "ba"),
            P("gz", "grp", "ba"),
            P("gz", "grp", "ba"),
            P("grp", ("gz", "ba")),
            P("grp", ("gz", "ba")),
            P("grp", ("gz", "ba")),
            P("grp", ("gz", "ba")),
            P("grp", ("gz", "ba")),
            P("grp", ("gz", "ba")),
            P("grp", ("gz", "ba")),
            P("grp", ("gz", "ba")),
            P("grp", ("gz", "ba")),
        ),
        check_vma=False,
    )
```

```python
import functools
import math

import jax
import jax.numpy as jnp
from jax import lax
from jax.experimental import pallas as pl
from jax.experimental.pallas import tpu as pltpu
from jax.sharding import PartitionSpec as P

learn_rate = 0.001
beta_first = 0.9
beta_second = 0.999
adam_epsilon = 1e-08
lanes = 128
MESH = pl.DeviceIdType.MESH
highest = lax.Precision.HIGHEST


def adam_step(weight, moment, square, gradient):
    moment_new = beta_first * moment + (1.0 - beta_first) * gradient
    square_new = beta_second * square + (1.0 - beta_second) * gradient * gradient
    updated = weight.astype(jnp.float32) - learn_rate * moment_new / (
        jnp.sqrt(square_new) + adam_epsilon
    )
    return (updated.astype(jnp.bfloat16), moment_new, square_new)


def nn(a, b, precision=None):
    return lax.dot_general(
        a, b, (((1,), (0,)), ((), ())), preferred_element_type=jnp.float32, precision=precision
    )


def nt(a, b, precision=None):
    return lax.dot_general(
        a, b, (((1,), (1,)), ((), ())), preferred_element_type=jnp.float32, precision=precision
    )


def tn(a, b, precision=None):
    return lax.dot_general(
        a, b, (((0,), (0,)), ((), ())), preferred_element_type=jnp.float32, precision=precision
    )


def split(values):
    high = values.astype(jnp.bfloat16)
    low = (values - high.astype(jnp.float32)).astype(jnp.bfloat16)
    return high, low


def iota(shape, axis):
    return lax.broadcasted_iota(jnp.int32, shape, axis)


def onehot(shape, offset, dtype=jnp.bfloat16):
    return (iota(shape, 0) + offset == iota(shape, 1)).astype(dtype)


def quotient(values, by):
    if by & (by - 1) == 0:
        return values >> (by.bit_length() - 1)
    return values // by


def remainder(values, by):
    if by & (by - 1) == 0:
        return values & (by - 1)
    return values % by


def step_kernel(slabs, halves, total_slices, *refs):
    inputs, refs = refs[:18], refs[18:]
    made, held, refs = refs[:13], refs[13:31], refs[31:]
    spectra_out, head_out, mid_out, out_out, in_out = (
        made[0],
        made[1:4],
        made[4:7],
        made[7:10],
        made[10:13],
    )
    (
        cos_t,
        trunk_in,
        trunk_mid,
        trunk_out,
        head_weight,
        band_width,
        band_weight,
        kernels,
        pair_bins,
        target,
        head_moment,
        head_square,
        in_moment,
        in_square,
        mid_moment,
        mid_square,
        out_moment,
        out_square,
    ) = held
    (
        fold_weight,
        cos_all,
        act_in,
        act_mid,
        hidden,
        pre_mid,
        pre_out,
        projection,
        fold_all,
        pair_table,
        gram_table,
        target_cot,
        band_power,
        power_send,
        power_recv,
        power_wide,
        bc_send,
        bc_recv,
        oc_send,
        oc_all,
        outer,
        load_sem,
        fold_load,
        cos_sems,
        fold_sems,
        fold_recv,
        side_sems,
        bc_sems,
        oc_sems,
    ) = refs
    group = lax.axis_index("grp")
    slab = lax.axis_index("gz")
    half = lax.axis_index("ba")
    count = slabs * halves
    me = slab * halves + half
    params, rows = cos_t.shape
    pairs, _, bands = target.shape
    slices, features, half_cells = head_weight.shape
    own = slices // halves
    cells = fold_weight.shape[2]
    padded = projection.shape[1]
    width = trunk_mid.shape[0]
    rows_half = slabs * rows
    rows_all = halves * rows_half
    solvers = slabs // 2
    quarter = slabs // 4
    solved = 2 * rows

    solves = (slab >= quarter) & (slab < quarter + solvers)
    below = slab < quarter
    solver = jnp.where(below, slab, jnp.where(solves, slab - quarter, slab - solvers))
    spot = 2 * solver + jnp.where(solves, 0, 1)
    solver_slab = solver + quarter
    outer_slab = jnp.where(solver < quarter, solver, solver + solvers)

    def exclusive(a, b):
        return a + b - 2 * (a & b)

    def slab_at(step):
        near = exclusive(solver, quotient(step, 2))
        far = jnp.where(near < quarter, near, near + solvers)
        if isinstance(step, int):
            return far if step % 2 else near + quarter
        return jnp.where(remainder(step, 2) == 1, far, near + quarter)

    def turn(first, last, body, backward=False):
        if last - first <= 16:
            for d in range(first, last):
                body(first + last - 1 - d if backward else d)
        else:

            def step(d, carry):
                body(first + last - 1 - d if backward else d)
                return carry

            lax.fori_loop(first, last, step, 0)

    start = pl.multiple_of(half * half_cells, half_cells)
    own_cells = pl.ds(start, half_cells)
    own_slices = pl.ds(half * own, own)
    loads = [
        pltpu.make_async_copy(
            source.at[:, :, own_cells] if i == 4 else source, kept, load_sem.at[i]
        )
        for i, (source, kept) in enumerate(zip(inputs, held))
    ]
    fold_copy = pltpu.make_async_copy(inputs[4].at[own_slices], fold_weight, fold_load)
    for i in (5, 6):
        loads[i].start()
    fold_copy.start()
    for i in (0, 7, 8, 1, 2, 3, 9):
        loads[i].start()

    barrier = pltpu.get_barrier_semaphore()

    def greet(d):
        pl.semaphore_signal(
            barrier,
            inc=1,
            device_id=(group, remainder(slab + d, slabs), half),
            device_id_type=MESH,
        )

    def side(shift):
        return (group, slab, lax.rem(half + shift, halves))

    turn(1, slabs, greet)
    for shift in range(1, halves):
        pl.semaphore_signal(barrier, inc=1, device_id=side(shift), device_id_type=MESH)

    loads[5].wait()
    loads[6].wait()
    triangle = iota((padded, bands), 0)
    column = iota((padded, bands), 1)
    widths = band_width[...].astype(jnp.float32).astype(jnp.bfloat16)
    ends = nt((triangle >= column).astype(jnp.bfloat16), widths).astype(jnp.int32)
    starts = nt((triangle > column).astype(jnp.bfloat16), widths).astype(jnp.int32)
    cell = iota((padded, cells), 1)
    for s in range(slices):
        member = (starts[:, s : s + 1] <= cell) & (cell < ends[:, s : s + 1])
        weighted = jnp.where(member, band_weight[s : s + 1, :], 0.0)
        total = jnp.maximum(jnp.sum(weighted, axis=1, keepdims=True), 1e-30)
        projection[s] = (weighted * (1.0 / total)).astype(jnp.bfloat16)
    fold_copy.wait()
    for k in range(own):
        fold = nt(projection[half * own + k], fold_weight[k])
        fold_all[half, slab, k] = fold.astype(jnp.bfloat16)
    loads[0].wait()
    cos_own = nt(onehot((rows, rows), 0), cos_t[...]).astype(jnp.bfloat16)
    cos_all[half, spot] = cos_own
    pl.semaphore_wait(barrier, slabs - 1 + halves - 1)

    def cos_copy(step):
        return pltpu.make_async_remote_copy(
            src_ref=cos_all.at[half, spot],
            dst_ref=cos_all.at[half, spot],
            send_sem=cos_sems.at[0],
            recv_sem=cos_sems.at[1],
            device_id=(group, slab_at(step), half),
            device_id_type=MESH,
        )

    def fold_send(step):
        return pltpu.make_async_remote_copy(
            src_ref=fold_all.at[half, slab],
            dst_ref=fold_all.at[half, slab],
            send_sem=fold_sems.at[0],
            recv_sem=fold_recv.at[slab],
            device_id=(group, exclusive(solver, step) + quarter, half),
            device_id_type=MESH,
        )

    def other_slabs(body):
        def at(step):
            pl.when(slab_at(step) != slab)(lambda: body(step))

        turn(0, slabs, at, True)

    other_slabs(lambda step: cos_copy(step).start())
    turn(1, solvers, lambda step: fold_send(step).start(), True)
    pl.when(jnp.logical_not(solves))(lambda: fold_send(0).start())
    for i in range(10, 18):
        loads[i].start()
    loads[4].start()

    for i in (7, 8):
        loads[i].wait()
    bins = kernels.shape[0]
    weights = 8.0 / math.sqrt(total_slices)
    for piece in range(2):
        chosen = (iota((bins, pairs), 0) == pair_bins[piece : piece + 1, :]).astype(jnp.float32)
        weights = weights * tn(kernels[...], chosen, highest)
    for p in range(pairs):
        pair_table[p] = jnp.broadcast_to(weights[:, p : p + 1], (total_slices, lanes))
    loads[9].wait()
    target_cot[0] = jnp.zeros_like(target_cot[0])
    block = math.gcd(total_slices, 16)
    for first in range(0, total_slices, block):

        def gather(p, sums):
            values = target[p]
            return tuple(
                old + pair_table[p, first + z : first + z + 1, :bands] * values
                for z, old in enumerate(sums)
            )

        sums = lax.fori_loop(
            0, pairs, gather, tuple(jnp.zeros((rows, bands), jnp.float32) for _ in range(block))
        )
        for z, values in enumerate(sums):
            target_cot[0, first + z, :, :bands] = values.astype(jnp.bfloat16)

    target_copy = pltpu.make_async_remote_copy(
        src_ref=target_cot.at[0],
        dst_ref=target_cot.at[1],
        send_sem=side_sems.at[0],
        recv_sem=side_sems.at[1],
        device_id=(group, solver_slab, half),
        device_id_type=MESH,
    )
    pl.when(jnp.logical_not(solves))(target_copy.start)

    for i in (1, 2, 3):
        loads[i].wait()

    def whole(ref, semaphore):
        return pltpu.make_async_copy(ref, ref, semaphore)

    def forward(part):
        cosmology = cos_all[part].reshape(rows_half, params)
        pre = nn(cosmology, trunk_in[...])
        act = (pre * jax.nn.sigmoid(pre)).astype(jnp.bfloat16)
        act_in[part] = act
        pre = nn(act, trunk_mid[...])
        pre_mid[part] = pre
        act = (pre * jax.nn.sigmoid(pre)).astype(jnp.bfloat16)
        act_mid[part] = act
        pre = nn(act, trunk_out[...])
        pre_out[part] = pre
        act = (pre * jax.nn.sigmoid(pre)).astype(jnp.bfloat16)
        hidden[part] = act

    def slope(values):
        sigmoid = jax.nn.sigmoid(values)
        return sigmoid * (1.0 + values * (1.0 - sigmoid))

    def side_copy(ref, sems, shift):
        return pltpu.make_async_remote_copy(
            src_ref=ref.at[half],
            dst_ref=ref.at[half],
            send_sem=sems.at[2],
            recv_sem=sems.at[2 + shift],
            device_id=side(shift),
            device_id_type=MESH,
        )

    def side_start(ref, sems):
        for shift in range(1, halves):
            side_copy(ref, sems, shift).start()

    def side_wait(ref, sems):
        for shift in range(1, halves):
            whole(ref.at[lax.rem(half + halves - shift, halves)], sems.at[2 + shift]).wait()

    whole(cos_all.at[half, pl.ds(0, slabs - 1)], cos_sems.at[1]).wait()
    side_start(cos_all, cos_sems)
    forward(half)

    my_rows = pl.ds(pl.multiple_of(solver * solved, solved), solved)

    def fold_side(j, shift):
        return pltpu.make_async_remote_copy(
            src_ref=fold_all.at[half, j],
            dst_ref=fold_all.at[half, j],
            send_sem=fold_sems.at[1],
            recv_sem=fold_sems.at[1 + shift],
            device_id=side(shift),
            device_id_type=MESH,
        )

    def bc_copy(step):
        return pltpu.make_async_remote_copy(
            src_ref=bc_send.at[slab_at(step)],
            dst_ref=bc_recv.at[half, solver],
            send_sem=bc_sems.at[0],
            recv_sem=bc_sems.at[1],
            device_id=(group, slab_at(step), half),
            device_id_type=MESH,
        )

    def oc_copy(step):
        return pltpu.make_async_remote_copy(
            src_ref=oc_send,
            dst_ref=oc_all.at[half, solver],
            send_sem=oc_sems.at[0],
            recv_sem=oc_sems.at[1],
            device_id=(group, slab_at(step), half),
            device_id_type=MESH,
        )

    power_copy = pltpu.make_async_remote_copy(
        src_ref=power_send.at[1],
        dst_ref=power_recv,
        send_sem=side_sems.at[2],
        recv_sem=side_sems.at[3],
        device_id=(group, outer_slab, half),
        device_id_type=MESH,
    )
    power_own = pltpu.make_async_copy(power_send.at[0], power_recv, side_sems.at[3])
    bc_own = pltpu.make_async_copy(bc_send.at[slab], bc_recv.at[half, solver], bc_sems.at[1])
    oc_own = pltpu.make_async_copy(oc_send, oc_all.at[half, solver], oc_sems.at[1])

    def solve():
        features_own = hidden[half, my_rows, :]

        def powers(part, j):
            for k in range(own):
                z = (j * halves + part) * own + k
                band_power[z] = nt(features_own, fold_all[part, j, k])

        for shift in range(1, halves):
            fold_side(slab, shift).start()
        powers(half, slab)
        for z in range(total_slices):
            both = jnp.sum(weights * weights[z : z + 1, :], axis=1, keepdims=True)
            gram_table[z] = jnp.broadcast_to(both, (total_slices, lanes))

        def piece(step):
            j = slab_at(step)
            pltpu.make_async_remote_copy(
                src_ref=fold_all.at[half, j],
                dst_ref=fold_all.at[half, j],
                send_sem=fold_sems.at[0],
                recv_sem=fold_recv.at[j],
                device_id=(group, j, half),
                device_id_type=MESH,
            ).wait_recv()
            for shift in range(1, halves):
                fold_side(j, shift).start()
            powers(half, j)

        turn(1, slabs, piece)
        for shift in range(1, halves):
            part = lax.rem(half + halves - shift, halves)
            whole(fold_all.at[part], fold_sems.at[1 + shift]).wait()
            turn(0, slabs, lambda j: powers(part, j))
        whole(target_cot.at[1], side_sems.at[1]).wait()

        def cots(z, carry):
            total = -jnp.concatenate([target_cot[0, z], target_cot[1, z]], axis=0).astype(
                jnp.float32
            )
            for other in range(total_slices):
                total = total + gram_table[z, other : other + 1, :padded] * band_power[other]
            bc_send[quotient(z, slices), remainder(z, slices)] = total.astype(jnp.bfloat16)
            return carry

        lax.fori_loop(0, total_slices, cots, 0)
        turn(1, slabs, lambda step: bc_copy(step).start(), True)
        bc_own.start()
        part = jnp.zeros((solved, features), jnp.float32)
        for z in range(total_slices):
            j, s = divmod(z, slices)
            part = part + nn(bc_send[j, s], fold_all[s // own, j, s % own])
        oc_send[...] = (part * slope(pre_out[half, my_rows, :])).astype(jnp.bfloat16)
        turn(1, slabs, lambda step: oc_copy(step).start(), True)
        oc_own.start()
        for z in range(total_slices):
            power = band_power[z].astype(jnp.bfloat16)
            power_send[0, z] = power[:rows]
            power_send[1, z] = power[rows:]
        power_copy.start()
        power_own.start()

    pl.when(solves)(solve)

    side_wait(cos_all, cos_sems)
    for shift in range(1, halves):
        forward(lax.rem(half + shift, halves))

    whole(power_recv, side_sems.at[3]).wait()
    power_wide[...] = power_recv[...].astype(jnp.float32)

    def predict(p, carry):
        total = pair_table[p, 0:1, :bands] * power_wide[0, :, :bands]
        for z in range(1, total_slices):
            total = total + pair_table[p, z : z + 1, :bands] * power_wide[z, :, :bands]
        spectra_out[p] = total
        return carry

    mid_columns = mid_moment.shape[0]
    out_columns = out_moment.shape[0]
    pick_mid = onehot((mid_columns, width), me * mid_columns)
    pick_out = onehot((out_columns, features), me * out_columns)
    mid_own = nt(pick_mid, trunk_mid[...])
    out_own = nt(pick_out, trunk_out[...])
    in_own = nt(trunk_in[...], pick_mid)
    mid_rows = nn(pick_mid, trunk_mid[...]).astype(jnp.bfloat16)
    in_columns = nt(pick_mid, trunk_in[...]).astype(jnp.bfloat16)
    cosmology = cos_all[...].reshape(rows_all, params)
    in_slope = slope(nt(in_columns, cosmology))
    cosmology_t = nt(onehot((params, params), 0), cosmology).astype(jnp.bfloat16)
    mid_slope = slope(pre_mid[...].reshape(rows_all, width))
    for i in (4, *range(10, 18)):
        loads[i].wait()

    whole(bc_recv.at[half], bc_sems.at[1]).wait()
    side_start(bc_recv, bc_sems)
    lax.fori_loop(0, pairs, predict, 0)
    side_wait(bc_recv, bc_sems)
    hidden_all = hidden[...].reshape(rows_all, features)
    for s in range(slices):
        cots = bc_recv[:, :, s].reshape(rows_all, padded)
        outer[s] = tn(hidden_all, cots).astype(jnp.bfloat16)
    whole(oc_all.at[half], oc_sems.at[1]).wait()
    side_start(oc_all, oc_sems)
    chunk_rows = 64

    def update_head(s):
        def step(i, carry):
            chunk = pl.ds(pl.multiple_of(i * chunk_rows, chunk_rows), chunk_rows)
            gradient = nn(outer[s, chunk, :], projection[s, :, own_cells])
            new, moment, square = adam_step(
                head_weight[s, chunk, :],
                head_moment[s, chunk, :],
                head_square[s, chunk, :],
                gradient,
            )
            head_out[0][s, chunk, :] = new
            head_out[1][s, chunk, :] = moment
            head_out[2][s, chunk, :] = square
            return carry

        lax.fori_loop(0, features // chunk_rows, step, 0)

    for s in range(slices):
        update_head(s)
    side_wait(oc_all, oc_sems)
    out_cot = oc_all[...].reshape(rows_all, features)
    mid_cot = (nt(out_cot, trunk_out[...]) * mid_slope).astype(jnp.bfloat16)
    out_cot_own = nt(pick_out, out_cot).astype(jnp.bfloat16)
    out_grad = nn(out_cot_own, act_mid[...].reshape(rows_all, width))
    mid_cot_own = nt(pick_mid, mid_cot).astype(jnp.bfloat16)
    mid_grad = nn(mid_cot_own, act_in[...].reshape(rows_all, width))
    in_cot_own = (nt(mid_rows, mid_cot) * in_slope).astype(jnp.bfloat16)
    in_grad = nt(cosmology_t, in_cot_own)
    for outs, own_weight, moment, square, gradient in (
        (mid_out, mid_own, mid_moment, mid_square, mid_grad),
        (out_out, out_own, out_moment, out_square, out_grad),
        (in_out, in_own, in_moment, in_square, in_grad),
    ):
        updated = adam_step(own_weight, moment[...], square[...], gradient)
        for out, value in zip(outs, updated):
            out[...] = value

    whole(cos_all.at[half, pl.ds(0, slabs - 1)], cos_sems.at[0]).wait()
    for shift in range(1, halves):
        for ref, sems in ((cos_all, cos_sems), (bc_recv, bc_sems), (oc_all, oc_sems)):
            whole(ref.at[half], sems.at[2]).wait()

    def sent_by_solver():
        whole(fold_all.at[half, pl.ds(0, solvers - 1)], fold_sems.at[0]).wait()
        for shift in range(1, halves):
            whole(fold_all.at[half], fold_sems.at[1]).wait()
        whole(bc_send.at[pl.ds(0, slabs - 1)], bc_sems.at[0]).wait()

        def step(i, carry):
            whole(oc_send, oc_sems.at[0]).wait()
            return carry

        lax.fori_loop(0, slabs - 1, step, 0)
        whole(power_send.at[1], side_sems.at[2]).wait()

    def sent_by_other():
        whole(fold_all.at[half, pl.ds(0, solvers)], fold_sems.at[0]).wait()
        whole(target_cot.at[0], side_sems.at[0]).wait()

    pl.when(solves)(sent_by_solver)
    pl.when(jnp.logical_not(solves))(sent_by_other)


def store_kernel(amount, *refs):
    sources, results, semaphores = refs[:amount], refs[amount : 2 * amount], refs[-1]
    stores = [
        pltpu.make_async_copy(source, result, semaphores.at[i])
        for i, (source, result) in enumerate(zip(sources, results))
    ]
    for store in stores:
        store.start()
    for store in stores:
        store.wait()


def shards(
    cosmology,
    trunk_in,
    trunk_mid,
    trunk_out,
    head_weight,
    band_width,
    band_weight,
    kernels,
    pair_bins,
    target,
    head_moment,
    head_square,
    in_moment,
    in_square,
    mid_moment,
    mid_square,
    out_moment,
    out_square,
):
    slabs = lax.axis_size("gz")
    halves = lax.axis_size("ba")
    count = slabs * halves
    rows, params = cosmology.shape
    pairs, bands = target.shape[1:]
    slices, features, cells = head_weight.shape
    width = trunk_mid.shape[0]
    rows_half = slabs * rows
    total_slices = slices * slabs
    own = slices // halves
    solvers = slabs // 2
    solved = 2 * rows
    padded = -(-bands // 8) * 8
    half_cells = cells // halves
    mid_columns = width // count
    out_columns = features // count
    bf16, f32 = jnp.bfloat16, jnp.float32
    hbm = pl.BlockSpec(memory_space=pltpu.HBM)
    vmem = pl.BlockSpec(memory_space=pltpu.VMEM)
    dma = pltpu.SemaphoreType.DMA
    inputs = (
        cosmology.T,
        trunk_in,
        trunk_mid,
        trunk_out,
        head_weight,
        band_width,
        band_weight,
        kernels,
        pair_bins.T,
        target.transpose(1, 0, 2),
        head_moment,
        head_square,
        in_moment,
        in_square,
        mid_moment.T,
        mid_square.T,
        out_moment.T,
        out_square.T,
    )
    inputs = tuple(pltpu.with_memory_space_constraint(a, pltpu.HBM) for a in inputs)
    out_shapes = [jax.ShapeDtypeStruct((pairs, rows, bands), f32)] + [
        jax.ShapeDtypeStruct(shape, dtype)
        for shape in (
            (slices, features, half_cells),
            (mid_columns, width),
            (out_columns, width),
            (params, mid_columns),
        )
        for dtype in (bf16, f32, f32)
    ]
    outs = pl.pallas_call(
        functools.partial(step_kernel, slabs, halves, total_slices),
        out_shape=[pltpu.VMEM(a.shape, a.dtype) for a in out_shapes],
        in_specs=[hbm] * len(inputs),
        out_specs=[vmem] * len(out_shapes),
        scratch_shapes=[
            pltpu.VMEM((slices, features, half_cells) if i == 4 else a.shape, a.dtype)
            for i, a in enumerate(inputs)
        ]
        + [
            pltpu.VMEM((own, features, cells), bf16),
            pltpu.VMEM((halves, slabs, rows, params), bf16),
            pltpu.VMEM((halves, rows_half, width), bf16),
            pltpu.VMEM((halves, rows_half, width), bf16),
            pltpu.VMEM((halves, rows_half, features), bf16),
            pltpu.VMEM((halves, rows_half, width), f32),
            pltpu.VMEM((halves, rows_half, features), f32),
            pltpu.VMEM((slices, padded, cells), bf16),
            pltpu.VMEM((halves, slabs, own, padded, features), bf16),
            pltpu.VMEM((pairs, total_slices, lanes), f32),
            pltpu.VMEM((total_slices, total_slices, lanes), f32),
            pltpu.VMEM((2, total_slices, rows, padded), bf16),
            pltpu.VMEM((total_slices, solved, padded), f32),
            pltpu.VMEM((2, total_slices, rows, padded), bf16),
            pltpu.VMEM((total_slices, rows, padded), bf16),
            pltpu.VMEM((total_slices, rows, padded), f32),
            pltpu.VMEM((slabs, slices, solved, padded), bf16),
            pltpu.VMEM((halves, solvers, slices, solved, padded), bf16),
            pltpu.VMEM((solved, features), bf16),
            pltpu.VMEM((halves, solvers, solved, features), bf16),
            pltpu.VMEM((slices, features, padded), bf16),
            dma((len(inputs),)),
            dma,
            dma((2 + halves,)),
            dma((1 + halves,)),
            dma((slabs,)),
            dma((4,)),
            dma((2 + halves,)),
            dma((2 + halves,)),
        ],
        compiler_params=pltpu.CompilerParams(
            collective_id=0, has_side_effects=True, vmem_limit_bytes=40 << 20
        ),
        name="step",
    )(*inputs)
    outs = pl.pallas_call(
        functools.partial(store_kernel, len(out_shapes)),
        out_shape=out_shapes,
        in_specs=[vmem] * len(out_shapes),
        out_specs=[hbm] * len(out_shapes),
        scratch_shapes=[dma((len(out_shapes),))],
        compiler_params=pltpu.CompilerParams(vmem_limit_bytes=16 << 20),
        name="store",
    )(*outs)
    spectra, head, mid, out, inner = outs[0], outs[1:4], outs[4:7], outs[7:10], outs[10:13]
    return (
        spectra.transpose(1, 0, 2),
        *head,
        *inner,
        *(a.T for a in mid),
        *(a.T for a in out),
    )


def solution(mesh):
    placed = (
        P(("grp", "gz", "ba"), None),
        P(),
        P(),
        P(),
        P("gz", None, None),
        P("gz", None),
        P("gz", None),
        P(),
        P(),
        P(("grp", "gz", "ba"), None, None),
        P("gz", None, "ba"),
        P("gz", None, "ba"),
        P(None, ("gz", "ba")),
        P(None, ("gz", "ba")),
        P(None, ("gz", "ba")),
        P(None, ("gz", "ba")),
        P(None, ("gz", "ba")),
        P(None, ("gz", "ba")),
    )
    return jax.shard_map(
        shards,
        mesh=mesh,
        in_specs=placed,
        out_specs=(
            P(("grp", "gz", "ba"), None, None),
            P("gz", "grp", "ba"),
            P("gz", "grp", "ba"),
            P("gz", "grp", "ba"),
            P("grp", ("gz", "ba")),
            P("grp", ("gz", "ba")),
            P("grp", ("gz", "ba")),
            P("grp", ("gz", "ba")),
            P("grp", ("gz", "ba")),
            P("grp", ("gz", "ba")),
            P("grp", ("gz", "ba")),
            P("grp", ("gz", "ba")),
            P("grp", ("gz", "ba")),
        ),
        check_vma=False,
    )
```

```python
import functools
import math

import jax
import jax.numpy as jnp
from jax import lax
from jax.experimental import pallas as pl
from jax.experimental.pallas import tpu as pltpu
from jax.sharding import PartitionSpec as P

learn_rate = 0.001
beta_first = 0.9
beta_second = 0.999
adam_epsilon = 1e-08
lanes = 128
MESH = pl.DeviceIdType.MESH
highest = lax.Precision.HIGHEST


def adam_step(weight, moment, square, gradient):
    moment_new = beta_first * moment + (1.0 - beta_first) * gradient
    square_new = beta_second * square + (1.0 - beta_second) * gradient * gradient
    updated = weight.astype(jnp.float32) - learn_rate * moment_new / (
        jnp.sqrt(square_new) + adam_epsilon
    )
    return (updated.astype(jnp.bfloat16), moment_new, square_new)


def nn(a, b, precision=None):
    return lax.dot_general(
        a, b, (((1,), (0,)), ((), ())), preferred_element_type=jnp.float32, precision=precision
    )


def nt(a, b, precision=None):
    return lax.dot_general(
        a, b, (((1,), (1,)), ((), ())), preferred_element_type=jnp.float32, precision=precision
    )


def tn(a, b, precision=None):
    return lax.dot_general(
        a, b, (((0,), (0,)), ((), ())), preferred_element_type=jnp.float32, precision=precision
    )


def split(values):
    high = values.astype(jnp.bfloat16)
    low = (values - high.astype(jnp.float32)).astype(jnp.bfloat16)
    return high, low


def iota(shape, axis):
    return lax.broadcasted_iota(jnp.int32, shape, axis)


def onehot(shape, offset, dtype=jnp.bfloat16):
    return (iota(shape, 0) + offset == iota(shape, 1)).astype(dtype)


def quotient(values, by):
    if by & (by - 1) == 0:
        return values >> (by.bit_length() - 1)
    return values // by


def remainder(values, by):
    if by & (by - 1) == 0:
        return values & (by - 1)
    return values % by


def step_kernel(slabs, halves, total_slices, *refs):
    inputs, refs = refs[:18], refs[18:]
    (
        spectra_out,
        outer,
        own_projection,
        head_weight,
        head_moment,
        head_square,
        in_moment,
        in_square,
        mid_moment,
        mid_square,
        out_moment,
        out_square,
        trunk_out,
        act_in,
        act_mid,
        oc_kept,
        mid_slope,
        in_slope,
        mid_own,
        out_own,
        in_own,
        mid_rows,
        cosmology_t,
        cos_t,
        trunk_in,
        trunk_mid,
        band_width,
        band_weight,
        kernels,
        pair_bins,
        target,
        fold_weight,
        cos_all,
        cos_pair,
        hidden,
        pre_mid,
        pre_own,
        projection,
        fold_all,
        pair_table,
        gram_table,
        target_cot,
        band_power,
        power_send,
        power_recv,
        power_wide,
        bc_send,
        bc_recv,
        oc_send,
        oc_all,
        load_sem,
        fold_load,
        cos_sems,
        fold_sems,
        fold_recv,
        side_recv,
        side_sems,
        bc_sems,
        oc_sems,
    ) = refs
    held = (
        cos_t,
        trunk_in,
        trunk_mid,
        trunk_out,
        head_weight,
        band_width,
        band_weight,
        kernels,
        pair_bins,
        target,
        head_moment,
        head_square,
        in_moment,
        in_square,
        mid_moment,
        mid_square,
        out_moment,
        out_square,
    )
    group = lax.axis_index("grp")
    slab = lax.axis_index("gz")
    half = lax.axis_index("ba")
    count = slabs * halves
    me = slab * halves + half
    params, rows = cos_t.shape
    pairs, _, bands = target.shape
    slices, features, half_cells = head_weight.shape
    own = slices // halves
    cells = fold_weight.shape[2]
    padded = projection.shape[1]
    width = trunk_mid.shape[0]
    rows_half = slabs * rows
    rows_all = halves * rows_half
    solvers = slabs // 2
    quarter = slabs // 4
    solved = 2 * rows

    solves = (slab >= quarter) & (slab < quarter + solvers)
    below = slab < quarter
    solver = jnp.where(below, slab, jnp.where(solves, slab - quarter, slab - solvers))
    spot = 2 * solver + jnp.where(solves, 0, 1)
    solver_slab = solver + quarter
    outer_slab = jnp.where(solver < quarter, solver, solver + solvers)

    def exclusive(a, b):
        return a + b - 2 * (a & b)

    def slab_at(step):
        near = exclusive(solver, quotient(step, 2))
        far = jnp.where(near < quarter, near, near + solvers)
        if isinstance(step, int):
            return far if step % 2 else near + quarter
        return jnp.where(remainder(step, 2) == 1, far, near + quarter)

    def turn(first, last, body, backward=False):
        if last - first <= 16:
            for d in range(first, last):
                body(first + last - 1 - d if backward else d)
        else:

            def step(d, carry):
                body(first + last - 1 - d if backward else d)
                return carry

            lax.fori_loop(first, last, step, 0)

    start = pl.multiple_of(half * half_cells, half_cells)
    own_cells = pl.ds(start, half_cells)
    own_slices = pl.ds(half * own, own)
    loads = [
        pltpu.make_async_copy(
            source.at[:, :, own_cells] if i == 4 else source, kept, load_sem.at[i]
        )
        for i, (source, kept) in enumerate(zip(inputs, held))
    ]
    fold_copy = pltpu.make_async_copy(inputs[4].at[own_slices], fold_weight, fold_load)
    for i in (5, 6):
        loads[i].start()
    fold_copy.start()
    for i in (0, 7, 8, 1, 2, 3, 9):
        loads[i].start()

    barrier = pltpu.get_barrier_semaphore()

    def greet(step):
        pl.semaphore_signal(
            barrier, inc=1, device_id=(group, slab_at(step), half), device_id_type=MESH
        )

    def side(shift):
        return (group, slab, lax.rem(half + shift, halves))

    def other_slabs(body):
        def at(step):
            pl.when(slab_at(step) != slab)(lambda: body(step))

        turn(0, slabs, at, True)

    other_slabs(greet)
    for shift in range(1, halves):
        pl.semaphore_signal(barrier, inc=1, device_id=side(shift), device_id_type=MESH)

    loads[5].wait()
    loads[6].wait()
    triangle = iota((padded, bands), 0)
    column = iota((padded, bands), 1)
    widths = band_width[...].astype(jnp.float32).astype(jnp.bfloat16)
    ends = nt((triangle >= column).astype(jnp.bfloat16), widths).astype(jnp.int32)
    starts = nt((triangle > column).astype(jnp.bfloat16), widths).astype(jnp.int32)
    cell = iota((padded, cells), 1)
    for s in range(slices):
        member = (starts[:, s : s + 1] <= cell) & (cell < ends[:, s : s + 1])
        weighted = jnp.where(member, band_weight[s : s + 1, :], 0.0)
        total = jnp.maximum(jnp.sum(weighted, axis=1, keepdims=True), 1e-30)
        projection[s] = (weighted * (1.0 / total)).astype(jnp.bfloat16)
    fold_copy.wait()
    for k in range(own):
        fold = nt(projection[half * own + k], fold_weight[k])
        fold_all[half, slab, k] = fold.astype(jnp.bfloat16)
    loads[0].wait()
    cos_own = nt(onehot((rows, rows), 0), cos_t[...]).astype(jnp.bfloat16)
    cos_all[half, spot] = cos_own
    cos_pair[0] = cos_own
    pl.semaphore_wait(barrier, slabs - 1 + halves - 1)

    def cos_copy(step):
        return pltpu.make_async_remote_copy(
            src_ref=cos_all.at[half, spot],
            dst_ref=cos_all.at[half, spot],
            send_sem=cos_sems.at[0],
            recv_sem=cos_sems.at[1],
            device_id=(group, slab_at(step), half),
            device_id_type=MESH,
        )

    def fold_send(step):
        return pltpu.make_async_remote_copy(
            src_ref=fold_all.at[half, slab],
            dst_ref=fold_all.at[half, slab],
            send_sem=fold_sems.at[0],
            recv_sem=fold_recv.at[slab],
            device_id=(group, exclusive(solver, step) + quarter, half),
            device_id_type=MESH,
        )

    cos_near = pltpu.make_async_remote_copy(
        src_ref=cos_pair.at[0],
        dst_ref=cos_pair.at[1],
        send_sem=side_sems.at[4],
        recv_sem=side_sems.at[5],
        device_id=(group, solver_slab, half),
        device_id_type=MESH,
    )
    pl.when(jnp.logical_not(solves))(cos_near.start)
    turn(1, solvers, lambda step: fold_send(step).start(), True)
    pl.when(jnp.logical_not(solves))(lambda: fold_send(0).start())
    other_slabs(lambda step: cos_copy(step).start())
    for i in range(10, 18):
        loads[i].start()
    loads[4].start()

    for i in (7, 8):
        loads[i].wait()
    bins = kernels.shape[0]
    weights = 8.0 / math.sqrt(total_slices)
    for piece in range(2):
        chosen = (iota((bins, pairs), 0) == pair_bins[piece : piece + 1, :]).astype(jnp.float32)
        weights = weights * tn(kernels[...], chosen, highest)
    for p in range(pairs):
        pair_table[p] = jnp.broadcast_to(weights[:, p : p + 1], (total_slices, lanes))
    loads[9].wait()
    target_cot[0] = jnp.zeros_like(target_cot[0])
    block = math.gcd(total_slices, 16)
    for first in range(0, total_slices, block):

        def gather(p, sums):
            values = target[p]
            return tuple(
                old + pair_table[p, first + z : first + z + 1, :bands] * values
                for z, old in enumerate(sums)
            )

        sums = lax.fori_loop(
            0, pairs, gather, tuple(jnp.zeros((rows, bands), jnp.float32) for _ in range(block))
        )
        for z, values in enumerate(sums):
            target_cot[0, first + z, :, :bands] = values.astype(jnp.bfloat16)

    target_copy = pltpu.make_async_remote_copy(
        src_ref=target_cot.at[0],
        dst_ref=target_cot.at[1],
        send_sem=side_sems.at[0],
        recv_sem=side_sems.at[1],
        device_id=(group, solver_slab, half),
        device_id_type=MESH,
    )
    pl.when(jnp.logical_not(solves))(target_copy.start)
    for s in range(slices):
        own_projection[s] = projection[s, :, own_cells]

    for i in (1, 2, 3):
        loads[i].wait()

    def whole(ref, semaphore):
        return pltpu.make_async_copy(ref, ref, semaphore)

    def forward(part):
        cosmology = cos_all[part].reshape(rows_half, params)
        pre = nn(cosmology, trunk_in[...])
        act = (pre * jax.nn.sigmoid(pre)).astype(jnp.bfloat16)
        act_in[part] = act
        pre = nn(act, trunk_mid[...])
        pre_mid[part] = pre
        act = (pre * jax.nn.sigmoid(pre)).astype(jnp.bfloat16)
        act_mid[part] = act
        pre = nn(act, trunk_out[...])
        act = (pre * jax.nn.sigmoid(pre)).astype(jnp.bfloat16)
        hidden[part] = act

    def slope(values):
        sigmoid = jax.nn.sigmoid(values)
        return sigmoid * (1.0 + values * (1.0 - sigmoid))

    def side_copy(ref, sems, shift):
        return pltpu.make_async_remote_copy(
            src_ref=ref.at[half],
            dst_ref=ref.at[half],
            send_sem=sems.at[2],
            recv_sem=sems.at[2 + shift],
            device_id=side(shift),
            device_id_type=MESH,
        )

    def side_start(ref, sems):
        for shift in range(1, halves):
            side_copy(ref, sems, shift).start()

    def side_wait(ref, sems):
        for shift in range(1, halves):
            whole(ref.at[lax.rem(half + halves - shift, halves)], sems.at[2 + shift]).wait()


    def fold_side(j, shift):
        return pltpu.make_async_remote_copy(
            src_ref=fold_all.at[half, j],
            dst_ref=fold_all.at[half, j],
            send_sem=fold_sems.at[1],
            recv_sem=side_recv.at[shift - 1, j],
            device_id=side(shift),
            device_id_type=MESH,
        )

    def bc_copy(step):
        return pltpu.make_async_remote_copy(
            src_ref=bc_send.at[slab_at(step)],
            dst_ref=bc_recv.at[half, solver],
            send_sem=bc_sems.at[0],
            recv_sem=bc_sems.at[1],
            device_id=(group, slab_at(step), half),
            device_id_type=MESH,
        )

    def oc_copy(step):
        return pltpu.make_async_remote_copy(
            src_ref=oc_send,
            dst_ref=oc_all.at[half, solver],
            send_sem=oc_sems.at[0],
            recv_sem=oc_sems.at[1],
            device_id=(group, slab_at(step), half),
            device_id_type=MESH,
        )

    def power_copy(part):
        return pltpu.make_async_remote_copy(
            src_ref=power_send.at[part],
            dst_ref=power_recv.at[part],
            send_sem=side_sems.at[2],
            recv_sem=side_sems.at[3],
            device_id=(group, outer_slab, half),
            device_id_type=MESH,
        )

    bc_own = pltpu.make_async_copy(bc_send.at[slab], bc_recv.at[half, solver], bc_sems.at[1])
    oc_own = pltpu.make_async_copy(oc_send, oc_all.at[half, solver], oc_sems.at[1])

    def solve():
        for shift in range(1, halves):
            fold_side(slab, shift).start()
        whole(cos_pair.at[1], side_sems.at[5]).wait()
        act = cos_pair[...].reshape(solved, params)
        for layer in (trunk_in, trunk_mid, trunk_out):
            pre = nn(act, layer[...])
            act = (pre * jax.nn.sigmoid(pre)).astype(jnp.bfloat16)
        pre_own[...] = pre
        features_own = act

        def powers(part, j):
            for k in range(own):
                z = (j * halves + part) * own + k
                power = nt(features_own, fold_all[part, j, k])
                band_power[z] = power
                power = power.astype(jnp.bfloat16)
                power_recv[part, j * own + k] = power[:rows]
                power_send[part, j * own + k] = power[rows:]

        powers(half, slab)
        for z in range(total_slices):
            both = jnp.sum(weights * weights[z : z + 1, :], axis=1, keepdims=True)
            gram_table[z] = jnp.broadcast_to(both, (total_slices, lanes))

        def piece(step):
            j = slab_at(step)
            pltpu.make_async_remote_copy(
                src_ref=fold_all.at[half, j],
                dst_ref=fold_all.at[half, j],
                send_sem=fold_sems.at[0],
                recv_sem=fold_recv.at[j],
                device_id=(group, j, half),
                device_id_type=MESH,
            ).wait_recv()
            for shift in range(1, halves):
                fold_side(j, shift).start()
            powers(half, j)

        turn(1, slabs, piece)
        power_copy(half).start()
        for shift in range(1, halves):
            part = lax.rem(half + halves - shift, halves)

            def side_piece(step):
                j = slab_at(step)
                whole(fold_all.at[part, j], side_recv.at[shift - 1, j]).wait()
                powers(part, j)

            turn(0, slabs, side_piece)
            power_copy(part).start()
        whole(target_cot.at[1], side_sems.at[1]).wait()

        def cots(j, carry):
            for s in range(slices):
                z = j * slices + s
                total = -jnp.concatenate([target_cot[0, z], target_cot[1, z]], axis=0).astype(
                    jnp.float32
                )
                for other in range(total_slices):
                    total = total + gram_table[z, other : other + 1, :padded] * band_power[other]
                bc_send[j, s] = total.astype(jnp.bfloat16)
            return carry

        lax.fori_loop(0, slabs, cots, 0)
        turn(1, slabs, lambda step: bc_copy(step).start(), True)
        bc_own.start()
        part = jnp.zeros((solved, features), jnp.float32)
        for z in range(total_slices):
            j, s = divmod(z, slices)
            part = part + nn(bc_send[j, s], fold_all[s // own, j, s % own])
        oc_send[...] = (part * slope(pre_own[...])).astype(jnp.bfloat16)
        turn(1, slabs, lambda step: oc_copy(step).start(), True)
        oc_own.start()

    pl.when(solves)(solve)

    whole(cos_all.at[half, pl.ds(0, slabs - 1)], cos_sems.at[1]).wait()
    side_start(cos_all, cos_sems)
    forward(half)
    side_wait(cos_all, cos_sems)
    for shift in range(1, halves):
        forward(lax.rem(half + shift, halves))

    group_pairs = max(n for n in range(1, 9) if pairs % n == 0)

    def predict(i, carry):
        for n in range(group_pairs):
            p = i * group_pairs + n
            total = None
            for z in range(total_slices):
                term = pair_table[p, z : z + 1, :bands] * power_wide[z, :, :bands]
                total = term if total is None else total + term
            spectra_out[p] = total
        return carry

    mid_columns = mid_moment.shape[0]
    out_columns = out_moment.shape[0]
    pick_mid = onehot((mid_columns, width), me * mid_columns)
    pick_out = onehot((out_columns, features), me * out_columns)
    mid_own[...] = nt(pick_mid, trunk_mid[...])
    out_own[...] = nt(pick_out, trunk_out[...])
    in_own[...] = nt(trunk_in[...], pick_mid)
    mid_rows[...] = nn(pick_mid, trunk_mid[...]).astype(jnp.bfloat16)
    in_columns = nt(pick_mid, trunk_in[...]).astype(jnp.bfloat16)
    cosmology = cos_all[...].reshape(rows_all, params)
    in_slope[...] = slope(nt(in_columns, cosmology))
    cosmology_t[...] = nt(onehot((params, params), 0), cosmology).astype(jnp.bfloat16)
    mid_slope[...] = slope(pre_mid[...].reshape(rows_all, width))
    for i in (4, *range(10, 18)):
        loads[i].wait()

    whole(bc_recv.at[half], bc_sems.at[1]).wait()
    side_start(bc_recv, bc_sems)
    whole(oc_all.at[half], oc_sems.at[1]).wait()
    side_start(oc_all, oc_sems)
    side_wait(bc_recv, bc_sems)
    hidden_all = hidden[...].reshape(rows_all, features)
    for s in range(slices):
        cots = bc_recv[:, :, s].reshape(rows_all, padded)
        outer[s] = tn(hidden_all, cots).astype(jnp.bfloat16)
    pl.when(jnp.logical_not(solves))(whole(power_recv, side_sems.at[3]).wait)
    for z in range(total_slices):
        j, s = divmod(z, slices)
        power_wide[z] = power_recv[s // own, j * own + s % own].astype(jnp.float32)
    lax.fori_loop(0, pairs // group_pairs, predict, 0)
    side_wait(oc_all, oc_sems)
    oc_kept[...] = oc_all[...].reshape(rows_all, features)

    whole(cos_all.at[half, pl.ds(0, slabs - 1)], cos_sems.at[0]).wait()
    for shift in range(1, halves):
        for ref, sems in ((cos_all, cos_sems), (bc_recv, bc_sems), (oc_all, oc_sems)):
            whole(ref.at[half], sems.at[2]).wait()

    def sent_by_solver():
        whole(fold_all.at[half, pl.ds(0, solvers - 1)], fold_sems.at[0]).wait()
        for shift in range(1, halves):
            whole(fold_all.at[half], fold_sems.at[1]).wait()
        whole(bc_send.at[pl.ds(0, slabs - 1)], bc_sems.at[0]).wait()

        def step(i, carry):
            whole(oc_send, oc_sems.at[0]).wait()
            return carry

        lax.fori_loop(0, slabs - 1, step, 0)
        whole(power_send, side_sems.at[2]).wait()

    def sent_by_other():
        whole(fold_all.at[half, pl.ds(0, solvers)], fold_sems.at[0]).wait()
        whole(target_cot.at[0], side_sems.at[0]).wait()
        whole(cos_pair.at[0], side_sems.at[4]).wait()

    pl.when(solves)(sent_by_solver)
    pl.when(jnp.logical_not(solves))(sent_by_other)


def update_kernel(slabs, halves, *refs):
    (
        spectra,
        outer,
        projection,
        head_weight,
        head_moment,
        head_square,
        in_moment,
        in_square,
        mid_moment,
        mid_square,
        out_moment,
        out_square,
        trunk_out,
        act_in,
        act_mid,
        oc_all,
        mid_slope,
        in_slope,
        mid_own,
        out_own,
        in_own,
        mid_rows,
        cosmology_t,
    ) = refs[:23]
    results, made, store_sem, head_sem = refs[23:36], refs[36:48], refs[48], refs[49]
    head_out, trunk_made = made[:3], made[3:]
    me = lax.axis_index("gz") * halves + lax.axis_index("ba")
    slices, features, _ = head_weight.shape
    rows_all, _ = oc_all.shape
    width = mid_rows.shape[1]
    stores = [
        pltpu.make_async_copy(source, result, store_sem.at[i])
        for i, (source, result) in enumerate(zip((spectra, *trunk_made), (results[0], *results[4:])))
    ]
    stores[0].start()
    chunk_rows = math.gcd(features, 256)
    chunks = features // chunk_rows

    def head_stores(s, i):
        chunk = pl.ds(pl.multiple_of(i * chunk_rows, chunk_rows), chunk_rows)
        return [
            pltpu.make_async_copy(
                head_out[k].at[s, chunk], results[1 + k].at[s, chunk], head_sem.at[k, s * chunks + i]
            )
            for k in range(3)
        ]

    def each(body):
        def step(n, carry):
            body(quotient(n, chunks), remainder(n, chunks))
            return carry

        lax.fori_loop(0, slices * chunks, step, 0)

    def update(s, i):
        chunk = pl.ds(pl.multiple_of(i * chunk_rows, chunk_rows), chunk_rows)
        gradient = nn(outer[s, chunk, :], projection[s])
        updated = adam_step(
            head_weight[s, chunk, :], head_moment[s, chunk, :], head_square[s, chunk, :], gradient
        )
        for out, value in zip(head_out, updated):
            out[s, chunk, :] = value
        for store in head_stores(s, i):
            store.start()

    each(update)
    pick_mid = onehot((mid_moment.shape[0], width), me * mid_moment.shape[0])
    pick_out = onehot((out_moment.shape[0], oc_all.shape[1]), me * out_moment.shape[0])
    out_cot = oc_all[...]
    mid_cot = (nt(out_cot, trunk_out[...]) * mid_slope[...]).astype(jnp.bfloat16)
    out_cot_own = nt(pick_out, out_cot).astype(jnp.bfloat16)
    out_grad = nn(out_cot_own, act_mid[...].reshape(rows_all, width))
    mid_cot_own = nt(pick_mid, mid_cot).astype(jnp.bfloat16)
    mid_grad = nn(mid_cot_own, act_in[...].reshape(rows_all, width))
    in_cot_own = (nt(mid_rows[...], mid_cot) * in_slope[...]).astype(jnp.bfloat16)
    in_grad = nt(cosmology_t[...], in_cot_own)
    for first, own_weight, moment, square, gradient in (
        (0, mid_own, mid_moment, mid_square, mid_grad),
        (3, out_own, out_moment, out_square, out_grad),
        (6, in_own, in_moment, in_square, in_grad),
    ):
        updated = adam_step(own_weight[...], moment[...], square[...], gradient)
        for k, value in enumerate(updated):
            trunk_made[first + k][...] = value
            stores[1 + first + k].start()
    for store in stores:
        store.wait()

    def wait(s, i):
        for store in head_stores(s, i):
            store.wait()

    each(wait)


def shards(
    cosmology,
    trunk_in,
    trunk_mid,
    trunk_out,
    head_weight,
    band_width,
    band_weight,
    kernels,
    pair_bins,
    target,
    head_moment,
    head_square,
    in_moment,
    in_square,
    mid_moment,
    mid_square,
    out_moment,
    out_square,
):
    slabs = lax.axis_size("gz")
    halves = lax.axis_size("ba")
    count = slabs * halves
    rows, params = cosmology.shape
    pairs, bands = target.shape[1:]
    slices, features, cells = head_weight.shape
    width = trunk_mid.shape[0]
    rows_half = slabs * rows
    total_slices = slices * slabs
    own = slices // halves
    solvers = slabs // 2
    solved = 2 * rows
    padded = -(-bands // 8) * 8
    half_cells = cells // halves
    mid_columns = width // count
    out_columns = features // count
    bf16, f32 = jnp.bfloat16, jnp.float32
    hbm = pl.BlockSpec(memory_space=pltpu.HBM)
    vmem = pl.BlockSpec(memory_space=pltpu.VMEM)
    dma = pltpu.SemaphoreType.DMA
    inputs = (
        cosmology.T,
        trunk_in,
        trunk_mid,
        trunk_out,
        head_weight,
        band_width,
        band_weight,
        kernels,
        pair_bins.T,
        target.transpose(1, 0, 2),
        head_moment,
        head_square,
        in_moment,
        in_square,
        mid_moment.T,
        mid_square.T,
        out_moment.T,
        out_square.T,
    )
    inputs = tuple(pltpu.with_memory_space_constraint(a, pltpu.HBM) for a in inputs)
    out_shapes = [jax.ShapeDtypeStruct((pairs, rows, bands), f32)] + [
        jax.ShapeDtypeStruct(shape, dtype)
        for shape in (
            (slices, features, half_cells),
            (mid_columns, width),
            (out_columns, width),
            (params, mid_columns),
        )
        for dtype in (bf16, f32, f32)
    ]
    kept = [
        ((pairs, rows, bands), f32),
        ((slices, features, padded), bf16),
        ((slices, padded, half_cells), bf16),
        ((slices, features, half_cells), bf16),
        *((inputs[i].shape, inputs[i].dtype) for i in (*range(10, 18), 3)),
        ((halves, rows_half, width), bf16),
        ((halves, rows_half, width), bf16),
        ((halves * rows_half, features), bf16),
        ((halves * rows_half, width), f32),
        ((mid_columns, halves * rows_half), f32),
        ((mid_columns, width), f32),
        ((out_columns, width), f32),
        ((params, mid_columns), f32),
        ((mid_columns, width), bf16),
        ((params, halves * rows_half), bf16),
    ]
    kept = pl.pallas_call(
        functools.partial(step_kernel, slabs, halves, total_slices),
        out_shape=[pltpu.VMEM(*a) for a in kept],
        in_specs=[hbm] * len(inputs),
        out_specs=[vmem] * len(kept),
        scratch_shapes=[
            pltpu.VMEM(inputs[i].shape, inputs[i].dtype) for i in (0, 1, 2, 5, 6, 7, 8, 9)
        ]
        + [
            pltpu.VMEM((own, features, cells), bf16),
            pltpu.VMEM((halves, slabs, rows, params), bf16),
            pltpu.VMEM((2, rows, params), bf16),
            pltpu.VMEM((halves, rows_half, features), bf16),
            pltpu.VMEM((halves, rows_half, width), f32),
            pltpu.VMEM((solved, features), f32),
            pltpu.VMEM((slices, padded, cells), bf16),
            pltpu.VMEM((halves, slabs, own, padded, features), bf16),
            pltpu.VMEM((pairs, total_slices, lanes), f32),
            pltpu.VMEM((total_slices, total_slices, lanes), f32),
            pltpu.VMEM((2, total_slices, rows, padded), bf16),
            pltpu.VMEM((total_slices, solved, padded), f32),
            pltpu.VMEM((halves, slabs * own, rows, padded), bf16),
            pltpu.VMEM((halves, slabs * own, rows, padded), bf16),
            pltpu.VMEM((total_slices, rows, padded), f32),
            pltpu.VMEM((slabs, slices, solved, padded), bf16),
            pltpu.VMEM((halves, solvers, slices, solved, padded), bf16),
            pltpu.VMEM((solved, features), bf16),
            pltpu.VMEM((halves, solvers, solved, features), bf16),
            dma((len(inputs),)),
            dma,
            dma((2 + halves,)),
            dma((2,)),
            dma((slabs,)),
            dma((halves - 1, slabs)),
            dma((6,)),
            dma((2 + halves,)),
            dma((2 + halves,)),
        ],
        compiler_params=pltpu.CompilerParams(
            collective_id=0, has_side_effects=True, vmem_limit_bytes=36 << 20
        ),
        name="step",
    )(*inputs)
    outs = pl.pallas_call(
        functools.partial(update_kernel, slabs, halves),
        out_shape=out_shapes,
        in_specs=[vmem] * len(kept),
        out_specs=[hbm] * len(out_shapes),
        scratch_shapes=[pltpu.VMEM(a.shape, a.dtype) for a in out_shapes[1:]]
        + [dma((len(out_shapes) - 3,)), dma((3, slices * (features // math.gcd(features, 256))))],
        compiler_params=pltpu.CompilerParams(vmem_limit_bytes=24 << 20),
        name="update",
    )(*kept)
    spectra, head, mid, out, inner = outs[0], outs[1:4], outs[4:7], outs[7:10], outs[10:13]
    return (
        spectra.transpose(1, 0, 2),
        *head,
        *inner,
        *(a.T for a in mid),
        *(a.T for a in out),
    )


def solution(mesh):
    placed = (
        P(("grp", "gz", "ba"), None),
        P(),
        P(),
        P(),
        P("gz", None, None),
        P("gz", None),
        P("gz", None),
        P(),
        P(),
        P(("grp", "gz", "ba"), None, None),
        P("gz", None, "ba"),
        P("gz", None, "ba"),
        P(None, ("gz", "ba")),
        P(None, ("gz", "ba")),
        P(None, ("gz", "ba")),
        P(None, ("gz", "ba")),
        P(None, ("gz", "ba")),
        P(None, ("gz", "ba")),
    )
    return jax.shard_map(
        shards,
        mesh=mesh,
        in_specs=placed,
        out_specs=(
            P(("grp", "gz", "ba"), None, None),
            P("gz", "grp", "ba"),
            P("gz", "grp", "ba"),
            P("gz", "grp", "ba"),
            P("grp", ("gz", "ba")),
            P("grp", ("gz", "ba")),
            P("grp", ("gz", "ba")),
            P("grp", ("gz", "ba")),
            P("grp", ("gz", "ba")),
            P("grp", ("gz", "ba")),
            P("grp", ("gz", "ba")),
            P("grp", ("gz", "ba")),
            P("grp", ("gz", "ba")),
        ),
        check_vma=False,
    )
```

```python
import functools
import math

import jax
import jax.numpy as jnp
from jax import lax
from jax.experimental import pallas as pl
from jax.experimental.pallas import tpu as pltpu
from jax.sharding import PartitionSpec as P

learn_rate = 0.001
beta_first = 0.9
beta_second = 0.999
adam_epsilon = 1e-08
lanes = 128
MESH = pl.DeviceIdType.MESH
highest = lax.Precision.HIGHEST


def adam_step(weight, moment, square, gradient):
    moment_new = beta_first * moment + (1.0 - beta_first) * gradient
    square_new = beta_second * square + (1.0 - beta_second) * gradient * gradient
    updated = weight.astype(jnp.float32) - learn_rate * moment_new / (
        jnp.sqrt(square_new) + adam_epsilon
    )
    return (updated.astype(jnp.bfloat16), moment_new, square_new)


def nn(a, b, precision=None):
    return lax.dot_general(
        a, b, (((1,), (0,)), ((), ())), preferred_element_type=jnp.float32, precision=precision
    )


def nt(a, b, precision=None):
    return lax.dot_general(
        a, b, (((1,), (1,)), ((), ())), preferred_element_type=jnp.float32, precision=precision
    )


def tn(a, b, precision=None):
    return lax.dot_general(
        a, b, (((0,), (0,)), ((), ())), preferred_element_type=jnp.float32, precision=precision
    )


def split(values):
    high = values.astype(jnp.bfloat16)
    low = (values - high.astype(jnp.float32)).astype(jnp.bfloat16)
    return high, low


def iota(shape, axis):
    return lax.broadcasted_iota(jnp.int32, shape, axis)


def onehot(shape, offset, dtype=jnp.bfloat16):
    return (iota(shape, 0) + offset == iota(shape, 1)).astype(dtype)


def quotient(values, by):
    if by & (by - 1) == 0:
        return values >> (by.bit_length() - 1)
    return values // by


def remainder(values, by):
    if by & (by - 1) == 0:
        return values & (by - 1)
    return values % by


def step_kernel(slabs, halves, total_slices, *refs):
    inputs, refs = refs[:18], refs[18:]
    (
        spectra_out,
        outer,
        own_projection,
        head_weight,
        head_moment,
        head_square,
        in_moment,
        in_square,
        mid_moment,
        mid_square,
        out_moment,
        out_square,
        trunk_out,
        act_in,
        act_mid,
        oc_kept,
        mid_slope,
        in_slope,
        mid_own,
        out_own,
        in_own,
        mid_rows,
        cosmology_t,
        cos_t,
        trunk_in,
        trunk_mid,
        band_width,
        band_weight,
        kernels,
        pair_bins,
        target,
        fold_weight,
        cos_all,
        cos_pair,
        hidden,
        pre_mid,
        pre_own,
        projection,
        fold_all,
        pair_table,
        gram_table,
        target_cot,
        band_power,
        power_send,
        power_recv,
        power_wide,
        bc_send,
        bc_recv,
        oc_send,
        oc_all,
        load_sem,
        fold_load,
        cos_sems,
        fold_sems,
        fold_recv,
        side_recv,
        side_sems,
        bc_sems,
        oc_sems,
    ) = refs
    held = (
        cos_t,
        trunk_in,
        trunk_mid,
        trunk_out,
        head_weight,
        band_width,
        band_weight,
        kernels,
        pair_bins,
        target,
        head_moment,
        head_square,
        in_moment,
        in_square,
        mid_moment,
        mid_square,
        out_moment,
        out_square,
    )
    group = lax.axis_index("grp")
    slab = lax.axis_index("gz")
    half = lax.axis_index("ba")
    count = slabs * halves
    me = slab * halves + half
    params, rows = cos_t.shape
    pairs, _, bands = target.shape
    slices, features, half_cells = head_weight.shape
    own = slices // halves
    cells = fold_weight.shape[2]
    padded = projection.shape[1]
    width = trunk_mid.shape[0]
    rows_half = slabs * rows
    rows_all = halves * rows_half
    solvers = slabs // 2
    quarter = slabs // 4
    solved = 2 * rows

    solves = (slab >= quarter) & (slab < quarter + solvers)
    below = slab < quarter
    solver = jnp.where(below, slab, jnp.where(solves, slab - quarter, slab - solvers))
    solver_slab = solver + quarter
    outer_slab = jnp.where(solver < quarter, solver, solver + solvers)

    def exclusive(a, b):
        return a + b - 2 * (a & b)

    def slab_at(step):
        near = exclusive(solver, quotient(step, 2))
        far = jnp.where(near < quarter, near, near + solvers)
        if isinstance(step, int):
            return far if step % 2 else near + quarter
        return jnp.where(remainder(step, 2) == 1, far, near + quarter)

    def turn(first, last, body, backward=False):
        if last - first <= 16:
            for d in range(first, last):
                body(first + last - 1 - d if backward else d)
        else:

            def step(d, carry):
                body(first + last - 1 - d if backward else d)
                return carry

            lax.fori_loop(first, last, step, 0)

    start = pl.multiple_of(half * half_cells, half_cells)
    own_cells = pl.ds(start, half_cells)
    own_slices = pl.ds(half * own, own)
    loads = [
        pltpu.make_async_copy(
            source.at[:, :, own_cells] if i == 4 else source, kept, load_sem.at[i]
        )
        for i, (source, kept) in enumerate(zip(inputs, held))
    ]
    fold_copy = pltpu.make_async_copy(inputs[4].at[own_slices], fold_weight, fold_load)
    for i in (5, 6):
        loads[i].start()
    fold_copy.start()
    for i in (0, 7, 8, 1, 2, 3, 9):
        loads[i].start()

    barrier = pltpu.get_barrier_semaphore()

    def greet(step):
        pl.semaphore_signal(
            barrier, inc=1, device_id=(group, slab_at(step), half), device_id_type=MESH
        )

    def side(shift):
        return (group, slab, lax.rem(half + shift, halves))

    pl.when(solves)(lambda: turn(1, slabs, greet, True))
    pl.when(jnp.logical_not(solves))(
        lambda: turn(0, solvers, lambda step: greet(2 * step), True)
    )
    for shift in range(1, halves):
        pl.semaphore_signal(barrier, inc=1, device_id=side(shift), device_id_type=MESH)

    loads[5].wait()
    loads[6].wait()
    triangle = iota((padded, bands), 0)
    column = iota((padded, bands), 1)
    widths = band_width[...].astype(jnp.float32).astype(jnp.bfloat16)
    ends = nt((triangle >= column).astype(jnp.bfloat16), widths).astype(jnp.int32)
    starts = nt((triangle > column).astype(jnp.bfloat16), widths).astype(jnp.int32)
    cell = iota((padded, cells), 1)
    for s in range(slices):
        member = (starts[:, s : s + 1] <= cell) & (cell < ends[:, s : s + 1])
        weighted = jnp.where(member, band_weight[s : s + 1, :], 0.0)
        total = jnp.maximum(jnp.sum(weighted, axis=1, keepdims=True), 1e-30)
        projection[s] = (weighted * (1.0 / total)).astype(jnp.bfloat16)
    fold_copy.wait()
    for k in range(own):
        fold = nt(projection[half * own + k], fold_weight[k])
        fold_all[half, slab, k] = fold.astype(jnp.bfloat16)
    loads[0].wait()
    cos_own = nt(onehot((rows, rows), 0), cos_t[...]).astype(jnp.bfloat16)
    cos_pair[0] = cos_own
    pl.semaphore_wait(barrier, jnp.where(solves, slabs - 1, solvers) + halves - 1)

    def cos_copy(step):
        return pltpu.make_async_remote_copy(
            src_ref=cos_pair,
            dst_ref=cos_all.at[half, pl.ds(2 * solver, 2)],
            send_sem=cos_sems.at[0],
            recv_sem=cos_sems.at[1],
            device_id=(group, slab_at(step), half),
            device_id_type=MESH,
        )

    def fold_send(step):
        return pltpu.make_async_remote_copy(
            src_ref=fold_all.at[half, slab],
            dst_ref=fold_all.at[half, slab],
            send_sem=fold_sems.at[0],
            recv_sem=fold_recv.at[slab],
            device_id=(group, exclusive(solver, step) + quarter, half),
            device_id_type=MESH,
        )

    cos_near = pltpu.make_async_remote_copy(
        src_ref=cos_pair.at[0],
        dst_ref=cos_pair.at[1],
        send_sem=side_sems.at[4],
        recv_sem=side_sems.at[5],
        device_id=(group, solver_slab, half),
        device_id_type=MESH,
    )
    pl.when(jnp.logical_not(solves))(cos_near.start)
    turn(1, solvers, lambda step: fold_send(step).start(), True)
    pl.when(jnp.logical_not(solves))(lambda: fold_send(0).start())
    for i in range(10, 18):
        loads[i].start()
    loads[4].start()

    for i in (7, 8):
        loads[i].wait()
    bins = kernels.shape[0]
    weights = 8.0 / math.sqrt(total_slices)
    for piece in range(2):
        chosen = (iota((bins, pairs), 0) == pair_bins[piece : piece + 1, :]).astype(jnp.float32)
        weights = weights * tn(kernels[...], chosen, highest)
    for p in range(pairs):
        pair_table[p] = jnp.broadcast_to(weights[:, p : p + 1], (total_slices, lanes))
    loads[9].wait()
    target_cot[0] = jnp.zeros_like(target_cot[0])
    block = math.gcd(total_slices, 16)
    for first in range(0, total_slices, block):

        def gather(p, sums):
            values = target[p]
            return tuple(
                old + pair_table[p, first + z : first + z + 1, :bands] * values
                for z, old in enumerate(sums)
            )

        sums = lax.fori_loop(
            0, pairs, gather, tuple(jnp.zeros((rows, bands), jnp.float32) for _ in range(block))
        )
        for z, values in enumerate(sums):
            target_cot[0, first + z, :, :bands] = values.astype(jnp.bfloat16)

    target_copy = pltpu.make_async_remote_copy(
        src_ref=target_cot.at[0],
        dst_ref=target_cot.at[1],
        send_sem=side_sems.at[0],
        recv_sem=side_sems.at[1],
        device_id=(group, solver_slab, half),
        device_id_type=MESH,
    )
    pl.when(jnp.logical_not(solves))(target_copy.start)
    for s in range(slices):
        own_projection[s] = projection[s, :, own_cells]

    for i in (1, 2, 3):
        loads[i].wait()

    def whole(ref, semaphore):
        return pltpu.make_async_copy(ref, ref, semaphore)

    def forward(part):
        cosmology = cos_all[part].reshape(rows_half, params)
        pre = nn(cosmology, trunk_in[...])
        act = (pre * jax.nn.sigmoid(pre)).astype(jnp.bfloat16)
        act_in[part] = act
        pre = nn(act, trunk_mid[...])
        pre_mid[part] = pre
        act = (pre * jax.nn.sigmoid(pre)).astype(jnp.bfloat16)
        act_mid[part] = act
        pre = nn(act, trunk_out[...])
        act = (pre * jax.nn.sigmoid(pre)).astype(jnp.bfloat16)
        hidden[part] = act

    def slope(values):
        sigmoid = jax.nn.sigmoid(values)
        return sigmoid * (1.0 + values * (1.0 - sigmoid))

    def side_copy(ref, sems, shift):
        return pltpu.make_async_remote_copy(
            src_ref=ref.at[half],
            dst_ref=ref.at[half],
            send_sem=sems.at[2],
            recv_sem=sems.at[2 + shift],
            device_id=side(shift),
            device_id_type=MESH,
        )

    def side_start(ref, sems):
        for shift in range(1, halves):
            side_copy(ref, sems, shift).start()

    def side_wait(ref, sems):
        for shift in range(1, halves):
            whole(ref.at[lax.rem(half + halves - shift, halves)], sems.at[2 + shift]).wait()


    def fold_side(j, shift):
        return pltpu.make_async_remote_copy(
            src_ref=fold_all.at[half, j],
            dst_ref=fold_all.at[half, j],
            send_sem=fold_sems.at[1],
            recv_sem=side_recv.at[shift - 1, j],
            device_id=side(shift),
            device_id_type=MESH,
        )

    def bc_copy(step):
        return pltpu.make_async_remote_copy(
            src_ref=bc_send.at[slab_at(step)],
            dst_ref=bc_recv.at[half, solver],
            send_sem=bc_sems.at[0],
            recv_sem=bc_sems.at[1],
            device_id=(group, slab_at(step), half),
            device_id_type=MESH,
        )

    def oc_copy(step):
        return pltpu.make_async_remote_copy(
            src_ref=oc_send,
            dst_ref=oc_all.at[half, solver],
            send_sem=oc_sems.at[0],
            recv_sem=oc_sems.at[1],
            device_id=(group, slab_at(step), half),
            device_id_type=MESH,
        )

    def power_copy(part):
        return pltpu.make_async_remote_copy(
            src_ref=power_send.at[part],
            dst_ref=power_recv.at[part],
            send_sem=side_sems.at[2],
            recv_sem=side_sems.at[3],
            device_id=(group, outer_slab, half),
            device_id_type=MESH,
        )

    bc_own = pltpu.make_async_copy(bc_send.at[slab], bc_recv.at[half, solver], bc_sems.at[1])
    oc_own = pltpu.make_async_copy(oc_send, oc_all.at[half, solver], oc_sems.at[1])

    def solve():
        for shift in range(1, halves):
            fold_side(slab, shift).start()
        whole(cos_pair.at[1], side_sems.at[5]).wait()
        turn(1, slabs, lambda step: cos_copy(step).start(), True)
        pltpu.make_async_copy(
            cos_pair, cos_all.at[half, pl.ds(2 * solver, 2)], cos_sems.at[1]
        ).start()
        act = cos_pair[...].reshape(solved, params)
        for layer in (trunk_in, trunk_mid, trunk_out):
            pre = nn(act, layer[...])
            act = (pre * jax.nn.sigmoid(pre)).astype(jnp.bfloat16)
        pre_own[...] = pre
        features_own = act

        def powers(part, j):
            for k in range(own):
                z = (j * halves + part) * own + k
                power = nt(features_own, fold_all[part, j, k])
                band_power[z] = power
                power = power.astype(jnp.bfloat16)
                power_recv[part, j * own + k] = power[:rows]
                power_send[part, j * own + k] = power[rows:]

        for z in range(total_slices):
            both = jnp.sum(weights * weights[z : z + 1, :], axis=1, keepdims=True)
            gram_table[z] = jnp.broadcast_to(both, (total_slices, lanes))

        def piece(step):
            j = slab_at(step)
            pltpu.make_async_remote_copy(
                src_ref=fold_all.at[half, j],
                dst_ref=fold_all.at[half, j],
                send_sem=fold_sems.at[0],
                recv_sem=fold_recv.at[j],
                device_id=(group, j, half),
                device_id_type=MESH,
            ).wait_recv()
            for shift in range(1, halves):
                fold_side(j, shift).start()

        turn(1, slabs, piece)
        turn(0, slabs, lambda j: powers(half, j))
        power_copy(half).start()
        for shift in range(1, halves):
            part = lax.rem(half + halves - shift, halves)

            def side_piece(step):
                j = slab_at(step)
                whole(fold_all.at[part, j], side_recv.at[shift - 1, j]).wait()

            turn(0, slabs, side_piece)
            turn(0, slabs, lambda j: powers(part, j))
            power_copy(part).start()
        whole(target_cot.at[1], side_sems.at[1]).wait()

        def cots(j, carry):
            for s in range(slices):
                z = j * slices + s
                total = -jnp.concatenate([target_cot[0, z], target_cot[1, z]], axis=0).astype(
                    jnp.float32
                )
                for other in range(total_slices):
                    total = total + gram_table[z, other : other + 1, :padded] * band_power[other]
                bc_send[j, s] = total.astype(jnp.bfloat16)
            return carry

        lax.fori_loop(0, slabs, cots, 0)
        turn(1, slabs, lambda step: bc_copy(step).start(), True)
        bc_own.start()
        part = jnp.zeros((solved, features), jnp.float32)
        for z in range(total_slices):
            j, s = divmod(z, slices)
            part = part + nn(bc_send[j, s], fold_all[s // own, j, s % own])
        oc_send[...] = (part * slope(pre_own[...])).astype(jnp.bfloat16)
        turn(1, slabs, lambda step: oc_copy(step).start(), True)
        oc_own.start()

    pl.when(solves)(solve)

    whole(cos_all.at[half], cos_sems.at[1]).wait()
    side_start(cos_all, cos_sems)
    forward(half)
    side_wait(cos_all, cos_sems)
    for shift in range(1, halves):
        forward(lax.rem(half + shift, halves))

    group_pairs = max(n for n in range(1, 9) if pairs % n == 0)

    def predict(i, carry):
        for n in range(group_pairs):
            p = i * group_pairs + n
            total = None
            for z in range(total_slices):
                term = pair_table[p, z : z + 1, :bands] * power_wide[z, :, :bands]
                total = term if total is None else total + term
            spectra_out[p] = total
        return carry

    mid_columns = mid_moment.shape[0]
    out_columns = out_moment.shape[0]
    pick_mid = onehot((mid_columns, width), me * mid_columns)
    pick_out = onehot((out_columns, features), me * out_columns)
    mid_own[...] = nt(pick_mid, trunk_mid[...])
    out_own[...] = nt(pick_out, trunk_out[...])
    in_own[...] = nt(trunk_in[...], pick_mid)
    mid_rows[...] = nn(pick_mid, trunk_mid[...]).astype(jnp.bfloat16)
    in_columns = nt(pick_mid, trunk_in[...]).astype(jnp.bfloat16)
    cosmology = cos_all[...].reshape(rows_all, params)
    in_slope[...] = slope(nt(in_columns, cosmology))
    cosmology_t[...] = nt(onehot((params, params), 0), cosmology).astype(jnp.bfloat16)
    mid_slope[...] = slope(pre_mid[...].reshape(rows_all, width))
    for i in (4, *range(10, 18)):
        loads[i].wait()

    pl.when(jnp.logical_not(solves))(whole(power_recv, side_sems.at[3]).wait)
    for z in range(total_slices):
        j, s = divmod(z, slices)
        power_wide[z] = power_recv[s // own, j * own + s % own].astype(jnp.float32)
    lax.fori_loop(0, pairs // group_pairs, predict, 0)
    whole(bc_recv.at[half], bc_sems.at[1]).wait()
    side_start(bc_recv, bc_sems)
    whole(oc_all.at[half], oc_sems.at[1]).wait()
    side_start(oc_all, oc_sems)
    side_wait(bc_recv, bc_sems)
    hidden_all = hidden[...].reshape(rows_all, features)
    for s in range(slices):
        cots = bc_recv[:, :, s].reshape(rows_all, padded)
        outer[s] = tn(hidden_all, cots).astype(jnp.bfloat16)
    side_wait(oc_all, oc_sems)
    oc_kept[...] = oc_all[...].reshape(rows_all, features)

    for shift in range(1, halves):
        for ref, sems in ((cos_all, cos_sems), (bc_recv, bc_sems), (oc_all, oc_sems)):
            whole(ref.at[half], sems.at[2]).wait()

    def sent_by_solver():
        whole(fold_all.at[half, pl.ds(0, solvers - 1)], fold_sems.at[0]).wait()
        for shift in range(1, halves):
            whole(fold_all.at[half], fold_sems.at[1]).wait()
        whole(bc_send.at[pl.ds(0, slabs - 1)], bc_sems.at[0]).wait()

        def step(i, carry):
            whole(oc_send, oc_sems.at[0]).wait()
            whole(cos_pair, cos_sems.at[0]).wait()
            return carry

        lax.fori_loop(0, slabs - 1, step, 0)
        whole(power_send, side_sems.at[2]).wait()

    def sent_by_other():
        whole(fold_all.at[half, pl.ds(0, solvers)], fold_sems.at[0]).wait()
        whole(target_cot.at[0], side_sems.at[0]).wait()
        whole(cos_pair.at[0], side_sems.at[4]).wait()

    pl.when(solves)(sent_by_solver)
    pl.when(jnp.logical_not(solves))(sent_by_other)


def update_kernel(slabs, halves, *refs):
    (
        spectra,
        outer,
        projection,
        head_weight,
        head_moment,
        head_square,
        in_moment,
        in_square,
        mid_moment,
        mid_square,
        out_moment,
        out_square,
        trunk_out,
        act_in,
        act_mid,
        oc_all,
        mid_slope,
        in_slope,
        mid_own,
        out_own,
        in_own,
        mid_rows,
        cosmology_t,
    ) = refs[:23]
    results, made, store_sem, head_sem = refs[23:36], refs[36:48], refs[48], refs[49]
    head_out, trunk_made = made[:3], made[3:]
    me = lax.axis_index("gz") * halves + lax.axis_index("ba")
    slices, features, _ = head_weight.shape
    rows_all, _ = oc_all.shape
    width = mid_rows.shape[1]
    stores = [
        pltpu.make_async_copy(source, result, store_sem.at[i])
        for i, (source, result) in enumerate(zip((spectra, *trunk_made), (results[0], *results[4:])))
    ]
    stores[0].start()
    chunk_rows = math.gcd(features, 256)
    chunks = features // chunk_rows

    def head_stores(s, i):
        chunk = pl.ds(pl.multiple_of(i * chunk_rows, chunk_rows), chunk_rows)
        return [
            pltpu.make_async_copy(
                head_out[k].at[s, chunk], results[1 + k].at[s, chunk], head_sem.at[k, s * chunks + i]
            )
            for k in range(3)
        ]

    def each(body):
        def step(n, carry):
            body(quotient(n, chunks), remainder(n, chunks))
            return carry

        lax.fori_loop(0, slices * chunks, step, 0)

    def update(s, i):
        chunk = pl.ds(pl.multiple_of(i * chunk_rows, chunk_rows), chunk_rows)
        gradient = nn(outer[s, chunk, :], projection[s])
        updated = adam_step(
            head_weight[s, chunk, :], head_moment[s, chunk, :], head_square[s, chunk, :], gradient
        )
        for out, value in zip(head_out, updated):
            out[s, chunk, :] = value
        for store in head_stores(s, i):
            store.start()

    each(update)
    pick_mid = onehot((mid_moment.shape[0], width), me * mid_moment.shape[0])
    pick_out = onehot((out_moment.shape[0], oc_all.shape[1]), me * out_moment.shape[0])
    out_cot = oc_all[...]
    mid_cot = (nt(out_cot, trunk_out[...]) * mid_slope[...]).astype(jnp.bfloat16)
    out_cot_own = nt(pick_out, out_cot).astype(jnp.bfloat16)
    out_grad = nn(out_cot_own, act_mid[...].reshape(rows_all, width))
    mid_cot_own = nt(pick_mid, mid_cot).astype(jnp.bfloat16)
    mid_grad = nn(mid_cot_own, act_in[...].reshape(rows_all, width))
    in_cot_own = (nt(mid_rows[...], mid_cot) * in_slope[...]).astype(jnp.bfloat16)
    in_grad = nt(cosmology_t[...], in_cot_own)
    for first, own_weight, moment, square, gradient in (
        (0, mid_own, mid_moment, mid_square, mid_grad),
        (3, out_own, out_moment, out_square, out_grad),
        (6, in_own, in_moment, in_square, in_grad),
    ):
        updated = adam_step(own_weight[...], moment[...], square[...], gradient)
        for k, value in enumerate(updated):
            trunk_made[first + k][...] = value
            stores[1 + first + k].start()
    for store in stores:
        store.wait()

    def wait(s, i):
        for store in head_stores(s, i):
            store.wait()

    each(wait)


def shards(
    cosmology,
    trunk_in,
    trunk_mid,
    trunk_out,
    head_weight,
    band_width,
    band_weight,
    kernels,
    pair_bins,
    target,
    head_moment,
    head_square,
    in_moment,
    in_square,
    mid_moment,
    mid_square,
    out_moment,
    out_square,
):
    slabs = lax.axis_size("gz")
    halves = lax.axis_size("ba")
    count = slabs * halves
    rows, params = cosmology.shape
    pairs, bands = target.shape[1:]
    slices, features, cells = head_weight.shape
    width = trunk_mid.shape[0]
    rows_half = slabs * rows
    total_slices = slices * slabs
    own = slices // halves
    solvers = slabs // 2
    solved = 2 * rows
    padded = -(-bands // 8) * 8
    half_cells = cells // halves
    mid_columns = width // count
    out_columns = features // count
    bf16, f32 = jnp.bfloat16, jnp.float32
    hbm = pl.BlockSpec(memory_space=pltpu.HBM)
    vmem = pl.BlockSpec(memory_space=pltpu.VMEM)
    dma = pltpu.SemaphoreType.DMA
    inputs = (
        cosmology.T,
        trunk_in,
        trunk_mid,
        trunk_out,
        head_weight,
        band_width,
        band_weight,
        kernels,
        pair_bins.T,
        target.transpose(1, 0, 2),
        head_moment,
        head_square,
        in_moment,
        in_square,
        mid_moment.T,
        mid_square.T,
        out_moment.T,
        out_square.T,
    )
    inputs = tuple(pltpu.with_memory_space_constraint(a, pltpu.HBM) for a in inputs)
    out_shapes = [jax.ShapeDtypeStruct((pairs, rows, bands), f32)] + [
        jax.ShapeDtypeStruct(shape, dtype)
        for shape in (
            (slices, features, half_cells),
            (mid_columns, width),
            (out_columns, width),
            (params, mid_columns),
        )
        for dtype in (bf16, f32, f32)
    ]
    kept = [
        ((pairs, rows, bands), f32),
        ((slices, features, padded), bf16),
        ((slices, padded, half_cells), bf16),
        ((slices, features, half_cells), bf16),
        *((inputs[i].shape, inputs[i].dtype) for i in (*range(10, 18), 3)),
        ((halves, rows_half, width), bf16),
        ((halves, rows_half, width), bf16),
        ((halves * rows_half, features), bf16),
        ((halves * rows_half, width), f32),
        ((mid_columns, halves * rows_half), f32),
        ((mid_columns, width), f32),
        ((out_columns, width), f32),
        ((params, mid_columns), f32),
        ((mid_columns, width), bf16),
        ((params, halves * rows_half), bf16),
    ]
    kept = pl.pallas_call(
        functools.partial(step_kernel, slabs, halves, total_slices),
        out_shape=[pltpu.VMEM(*a) for a in kept],
        in_specs=[hbm] * len(inputs),
        out_specs=[vmem] * len(kept),
        scratch_shapes=[
            pltpu.VMEM(inputs[i].shape, inputs[i].dtype) for i in (0, 1, 2, 5, 6, 7, 8, 9)
        ]
        + [
            pltpu.VMEM((own, features, cells), bf16),
            pltpu.VMEM((halves, slabs, rows, params), bf16),
            pltpu.VMEM((2, rows, params), bf16),
            pltpu.VMEM((halves, rows_half, features), bf16),
            pltpu.VMEM((halves, rows_half, width), f32),
            pltpu.VMEM((solved, features), f32),
            pltpu.VMEM((slices, padded, cells), bf16),
            pltpu.VMEM((halves, slabs, own, padded, features), bf16),
            pltpu.VMEM((pairs, total_slices, lanes), f32),
            pltpu.VMEM((total_slices, total_slices, lanes), f32),
            pltpu.VMEM((2, total_slices, rows, padded), bf16),
            pltpu.VMEM((total_slices, solved, padded), f32),
            pltpu.VMEM((halves, slabs * own, rows, padded), bf16),
            pltpu.VMEM((halves, slabs * own, rows, padded), bf16),
            pltpu.VMEM((total_slices, rows, padded), f32),
            pltpu.VMEM((slabs, slices, solved, padded), bf16),
            pltpu.VMEM((halves, solvers, slices, solved, padded), bf16),
            pltpu.VMEM((solved, features), bf16),
            pltpu.VMEM((halves, solvers, solved, features), bf16),
            dma((len(inputs),)),
            dma,
            dma((2 + halves,)),
            dma((2,)),
            dma((slabs,)),
            dma((halves - 1, slabs)),
            dma((6,)),
            dma((2 + halves,)),
            dma((2 + halves,)),
        ],
        compiler_params=pltpu.CompilerParams(
            collective_id=0, has_side_effects=True, vmem_limit_bytes=36 << 20
        ),
        name="step",
    )(*inputs)
    outs = pl.pallas_call(
        functools.partial(update_kernel, slabs, halves),
        out_shape=out_shapes,
        in_specs=[vmem] * len(kept),
        out_specs=[hbm] * len(out_shapes),
        scratch_shapes=[pltpu.VMEM(a.shape, a.dtype) for a in out_shapes[1:]]
        + [dma((len(out_shapes) - 3,)), dma((3, slices * (features // math.gcd(features, 256))))],
        compiler_params=pltpu.CompilerParams(vmem_limit_bytes=24 << 20),
        name="update",
    )(*kept)
    spectra, head, mid, out, inner = outs[0], outs[1:4], outs[4:7], outs[7:10], outs[10:13]
    return (
        spectra.transpose(1, 0, 2),
        *head,
        *inner,
        *(a.T for a in mid),
        *(a.T for a in out),
    )


def solution(mesh):
    placed = (
        P(("grp", "gz", "ba"), None),
        P(),
        P(),
        P(),
        P("gz", None, None),
        P("gz", None),
        P("gz", None),
        P(),
        P(),
        P(("grp", "gz", "ba"), None, None),
        P("gz", None, "ba"),
        P("gz", None, "ba"),
        P(None, ("gz", "ba")),
        P(None, ("gz", "ba")),
        P(None, ("gz", "ba")),
        P(None, ("gz", "ba")),
        P(None, ("gz", "ba")),
        P(None, ("gz", "ba")),
    )
    return jax.shard_map(
        shards,
        mesh=mesh,
        in_specs=placed,
        out_specs=(
            P(("grp", "gz", "ba"), None, None),
            P("gz", "grp", "ba"),
            P("gz", "grp", "ba"),
            P("gz", "grp", "ba"),
            P("grp", ("gz", "ba")),
            P("grp", ("gz", "ba")),
            P("grp", ("gz", "ba")),
            P("grp", ("gz", "ba")),
            P("grp", ("gz", "ba")),
            P("grp", ("gz", "ba")),
            P("grp", ("gz", "ba")),
            P("grp", ("gz", "ba")),
            P("grp", ("gz", "ba")),
        ),
        check_vma=False,
    )
```

```python
import functools
import math

import jax
import jax.numpy as jnp
from jax import lax
from jax.experimental import pallas as pl
from jax.experimental.pallas import tpu as pltpu
from jax.sharding import PartitionSpec as P

learn_rate = 0.001
beta_first = 0.9
beta_second = 0.999
adam_epsilon = 1e-08
lanes = 128
MESH = pl.DeviceIdType.MESH
highest = lax.Precision.HIGHEST


def adam_step(weight, moment, square, gradient):
    moment_new = beta_first * moment + (1.0 - beta_first) * gradient
    square_new = beta_second * square + (1.0 - beta_second) * gradient * gradient
    updated = weight.astype(jnp.float32) - learn_rate * moment_new / (
        jnp.sqrt(square_new) + adam_epsilon
    )
    return (updated.astype(jnp.bfloat16), moment_new, square_new)


def nn(a, b, precision=None):
    return lax.dot_general(
        a, b, (((1,), (0,)), ((), ())), preferred_element_type=jnp.float32, precision=precision
    )


def nt(a, b, precision=None):
    return lax.dot_general(
        a, b, (((1,), (1,)), ((), ())), preferred_element_type=jnp.float32, precision=precision
    )


def tn(a, b, precision=None):
    return lax.dot_general(
        a, b, (((0,), (0,)), ((), ())), preferred_element_type=jnp.float32, precision=precision
    )


def split(values):
    high = values.astype(jnp.bfloat16)
    low = (values - high.astype(jnp.float32)).astype(jnp.bfloat16)
    return high, low


def iota(shape, axis):
    return lax.broadcasted_iota(jnp.int32, shape, axis)


def onehot(shape, offset, dtype=jnp.bfloat16):
    return (iota(shape, 0) + offset == iota(shape, 1)).astype(dtype)


def quotient(values, by):
    if by & (by - 1) == 0:
        return values >> (by.bit_length() - 1)
    return values // by


def remainder(values, by):
    if by & (by - 1) == 0:
        return values & (by - 1)
    return values % by


def step_kernel(slabs, halves, total_slices, *refs):
    inputs, refs = refs[:18], refs[18:]
    (
        spectra_out,
        outer,
        own_projection,
        head_weight,
        head_moment,
        head_square,
        in_moment,
        in_square,
        mid_moment,
        mid_square,
        out_moment,
        out_square,
        trunk_out,
        act_in,
        act_mid,
        oc_kept,
        mid_slope,
        in_slope,
        mid_own,
        out_own,
        in_own,
        mid_rows,
        cosmology_t,
        early_new,
        early_moment,
        early_square,
        cos_t,
        trunk_in,
        trunk_mid,
        band_width,
        band_weight,
        kernels,
        pair_bins,
        target,
        fold_weight,
        cos_all,
        cos_pair,
        hidden,
        pre_mid,
        pre_own,
        projection,
        fold_all,
        pair_table,
        gram_table,
        target_cot,
        band_power,
        power_send,
        power_recv,
        power_wide,
        bc_send,
        bc_recv,
        oc_send,
        oc_all,
        load_sem,
        fold_load,
        cos_sems,
        fold_sems,
        fold_recv,
        side_recv,
        side_sems,
        bc_sems,
        oc_sems,
    ) = refs
    held = (
        cos_t,
        trunk_in,
        trunk_mid,
        trunk_out,
        head_weight,
        band_width,
        band_weight,
        kernels,
        pair_bins,
        target,
        head_moment,
        head_square,
        in_moment,
        in_square,
        mid_moment,
        mid_square,
        out_moment,
        out_square,
    )
    group = lax.axis_index("grp")
    slab = lax.axis_index("gz")
    half = lax.axis_index("ba")
    count = slabs * halves
    me = slab * halves + half
    params, rows = cos_t.shape
    pairs, _, bands = target.shape
    slices, features, half_cells = head_weight.shape
    own = slices // halves
    cells = fold_weight.shape[2]
    padded = projection.shape[1]
    width = trunk_mid.shape[0]
    rows_half = slabs * rows
    rows_all = halves * rows_half
    solvers = slabs // 2
    quarter = slabs // 4
    solved = 2 * rows

    solves = (slab >= quarter) & (slab < quarter + solvers)
    below = slab < quarter
    solver = jnp.where(below, slab, jnp.where(solves, slab - quarter, slab - solvers))
    solver_slab = solver + quarter
    outer_slab = jnp.where(solver < quarter, solver, solver + solvers)

    def exclusive(a, b):
        return a + b - 2 * (a & b)

    def slab_at(step):
        near = exclusive(solver, quotient(step, 2))
        far = jnp.where(near < quarter, near, near + solvers)
        if isinstance(step, int):
            return far if step % 2 else near + quarter
        return jnp.where(remainder(step, 2) == 1, far, near + quarter)

    def turn(first, last, body, backward=False):
        if last - first <= 16:
            for d in range(first, last):
                body(first + last - 1 - d if backward else d)
        else:

            def step(d, carry):
                body(first + last - 1 - d if backward else d)
                return carry

            lax.fori_loop(first, last, step, 0)

    start = pl.multiple_of(half * half_cells, half_cells)
    own_cells = pl.ds(start, half_cells)
    own_slices = pl.ds(half * own, own)
    loads = [
        pltpu.make_async_copy(
            source.at[:, :, own_cells] if i == 4 else source, kept, load_sem.at[i]
        )
        for i, (source, kept) in enumerate(zip(inputs, held))
    ]
    fold_copy = pltpu.make_async_copy(inputs[4].at[own_slices], fold_weight, fold_load)
    for i in (5, 6):
        loads[i].start()
    fold_copy.start()
    for i in (0, 7, 8, 1, 2, 3, 9):
        loads[i].start()

    barrier = pltpu.get_barrier_semaphore()

    def greet(step):
        pl.semaphore_signal(
            barrier, inc=1, device_id=(group, slab_at(step), half), device_id_type=MESH
        )

    def side(shift):
        return (group, slab, lax.rem(half + shift, halves))

    pl.when(solves)(lambda: turn(1, slabs, greet, True))
    pl.when(jnp.logical_not(solves))(
        lambda: turn(0, solvers, lambda step: greet(2 * step), True)
    )
    for shift in range(1, halves):
        pl.semaphore_signal(barrier, inc=1, device_id=side(shift), device_id_type=MESH)

    loads[5].wait()
    loads[6].wait()
    triangle = iota((padded, bands), 0)
    column = iota((padded, bands), 1)
    widths = band_width[...].astype(jnp.float32).astype(jnp.bfloat16)
    ends = nt((triangle >= column).astype(jnp.bfloat16), widths).astype(jnp.int32)
    starts = nt((triangle > column).astype(jnp.bfloat16), widths).astype(jnp.int32)
    cell = iota((padded, cells), 1)
    for s in range(slices):
        member = (starts[:, s : s + 1] <= cell) & (cell < ends[:, s : s + 1])
        weighted = jnp.where(member, band_weight[s : s + 1, :], 0.0)
        total = jnp.maximum(jnp.sum(weighted, axis=1, keepdims=True), 1e-30)
        projection[s] = (weighted * (1.0 / total)).astype(jnp.bfloat16)
    fold_copy.wait()
    for k in range(own):
        fold = nt(projection[half * own + k], fold_weight[k])
        fold_all[half, slab, k] = fold.astype(jnp.bfloat16)
    loads[0].wait()
    cos_own = nt(onehot((rows, rows), 0), cos_t[...]).astype(jnp.bfloat16)
    cos_pair[0] = cos_own
    pl.semaphore_wait(barrier, jnp.where(solves, slabs - 1, solvers) + halves - 1)

    def cos_copy(step):
        return pltpu.make_async_remote_copy(
            src_ref=cos_pair,
            dst_ref=cos_all.at[half, pl.ds(2 * solver, 2)],
            send_sem=cos_sems.at[0],
            recv_sem=cos_sems.at[1],
            device_id=(group, slab_at(step), half),
            device_id_type=MESH,
        )

    def fold_send(step):
        return pltpu.make_async_remote_copy(
            src_ref=fold_all.at[half, slab],
            dst_ref=fold_all.at[half, slab],
            send_sem=fold_sems.at[0],
            recv_sem=fold_recv.at[slab],
            device_id=(group, exclusive(solver, step) + quarter, half),
            device_id_type=MESH,
        )

    cos_near = pltpu.make_async_remote_copy(
        src_ref=cos_pair.at[0],
        dst_ref=cos_pair.at[1],
        send_sem=side_sems.at[4],
        recv_sem=side_sems.at[5],
        device_id=(group, solver_slab, half),
        device_id_type=MESH,
    )
    pl.when(jnp.logical_not(solves))(cos_near.start)
    turn(1, solvers, lambda step: fold_send(step).start(), True)
    pl.when(jnp.logical_not(solves))(lambda: fold_send(0).start())
    for i in range(10, 18):
        loads[i].start()
    loads[4].start()

    for i in (7, 8):
        loads[i].wait()
    bins = kernels.shape[0]
    weights = 8.0 / math.sqrt(total_slices)
    for piece in range(2):
        chosen = (iota((bins, pairs), 0) == pair_bins[piece : piece + 1, :]).astype(jnp.float32)
        weights = weights * tn(kernels[...], chosen, highest)
    for p in range(pairs):
        pair_table[p] = jnp.broadcast_to(weights[:, p : p + 1], (total_slices, lanes))
    loads[9].wait()
    target_cot[0] = jnp.zeros_like(target_cot[0])
    block = math.gcd(total_slices, 16)
    for first in range(0, total_slices, block):

        def gather(p, sums):
            values = target[p]
            return tuple(
                old + pair_table[p, first + z : first + z + 1, :bands] * values
                for z, old in enumerate(sums)
            )

        sums = lax.fori_loop(
            0, pairs, gather, tuple(jnp.zeros((rows, bands), jnp.float32) for _ in range(block))
        )
        for z, values in enumerate(sums):
            target_cot[0, first + z, :, :bands] = values.astype(jnp.bfloat16)

    target_copy = pltpu.make_async_remote_copy(
        src_ref=target_cot.at[0],
        dst_ref=target_cot.at[1],
        send_sem=side_sems.at[0],
        recv_sem=side_sems.at[1],
        device_id=(group, solver_slab, half),
        device_id_type=MESH,
    )
    pl.when(jnp.logical_not(solves))(target_copy.start)
    for s in range(slices):
        own_projection[s] = projection[s, :, own_cells]

    for i in (1, 2, 3):
        loads[i].wait()

    def whole(ref, semaphore):
        return pltpu.make_async_copy(ref, ref, semaphore)

    def forward(part):
        cosmology = cos_all[part].reshape(rows_half, params)
        pre = nn(cosmology, trunk_in[...])
        act = (pre * jax.nn.sigmoid(pre)).astype(jnp.bfloat16)
        act_in[part] = act
        pre = nn(act, trunk_mid[...])
        pre_mid[part] = pre
        act = (pre * jax.nn.sigmoid(pre)).astype(jnp.bfloat16)
        act_mid[part] = act
        pre = nn(act, trunk_out[...])
        act = (pre * jax.nn.sigmoid(pre)).astype(jnp.bfloat16)
        hidden[part] = act

    def slope(values):
        sigmoid = jax.nn.sigmoid(values)
        return sigmoid * (1.0 + values * (1.0 - sigmoid))

    def side_copy(ref, sems, shift):
        return pltpu.make_async_remote_copy(
            src_ref=ref.at[half],
            dst_ref=ref.at[half],
            send_sem=sems.at[2],
            recv_sem=sems.at[2 + shift],
            device_id=side(shift),
            device_id_type=MESH,
        )

    def side_start(ref, sems):
        for shift in range(1, halves):
            side_copy(ref, sems, shift).start()

    def side_wait(ref, sems):
        for shift in range(1, halves):
            whole(ref.at[lax.rem(half + halves - shift, halves)], sems.at[2 + shift]).wait()


    def fold_side(j, shift):
        return pltpu.make_async_remote_copy(
            src_ref=fold_all.at[half, j],
            dst_ref=fold_all.at[half, j],
            send_sem=fold_sems.at[1],
            recv_sem=side_recv.at[shift - 1],
            device_id=side(shift),
            device_id_type=MESH,
        )

    def bc_copy(step):
        return pltpu.make_async_remote_copy(
            src_ref=bc_send.at[slab_at(step)],
            dst_ref=bc_recv.at[half, solver],
            send_sem=bc_sems.at[0],
            recv_sem=bc_sems.at[1],
            device_id=(group, slab_at(step), half),
            device_id_type=MESH,
        )

    def oc_copy(step):
        return pltpu.make_async_remote_copy(
            src_ref=oc_send,
            dst_ref=oc_all.at[half, solver],
            send_sem=oc_sems.at[0],
            recv_sem=oc_sems.at[1],
            device_id=(group, slab_at(step), half),
            device_id_type=MESH,
        )

    def power_copy(part):
        return pltpu.make_async_remote_copy(
            src_ref=power_send.at[part],
            dst_ref=power_recv.at[part],
            send_sem=side_sems.at[2],
            recv_sem=side_sems.at[3],
            device_id=(group, outer_slab, half),
            device_id_type=MESH,
        )

    bc_own = pltpu.make_async_copy(bc_send.at[slab], bc_recv.at[half, solver], bc_sems.at[1])
    oc_own = pltpu.make_async_copy(oc_send, oc_all.at[half, solver], oc_sems.at[1])

    def solve():
        for shift in range(1, halves):
            fold_side(slab, shift).start()
        whole(cos_pair.at[1], side_sems.at[5]).wait()
        turn(1, slabs, lambda step: cos_copy(step).start(), True)
        pltpu.make_async_copy(
            cos_pair, cos_all.at[half, pl.ds(2 * solver, 2)], cos_sems.at[1]
        ).start()
        act = cos_pair[...].reshape(solved, params)
        for layer in (trunk_in, trunk_mid, trunk_out):
            pre = nn(act, layer[...])
            act = (pre * jax.nn.sigmoid(pre)).astype(jnp.bfloat16)
        pre_own[...] = pre
        features_own = act

        def powers(part, j):
            for k in range(own):
                z = (j * halves + part) * own + k
                power = nt(features_own, fold_all[part, j, k])
                band_power[z] = power
                power = power.astype(jnp.bfloat16)
                power_recv[part, j * own + k] = power[:rows]
                power_send[part, j * own + k] = power[rows:]

        for z in range(total_slices):
            both = jnp.sum(weights * weights[z : z + 1, :], axis=1, keepdims=True)
            gram_table[z] = jnp.broadcast_to(both, (total_slices, lanes))

        def piece(step):
            j = slab_at(step)
            pltpu.make_async_remote_copy(
                src_ref=fold_all.at[half, j],
                dst_ref=fold_all.at[half, j],
                send_sem=fold_sems.at[0],
                recv_sem=fold_recv.at[j],
                device_id=(group, j, half),
                device_id_type=MESH,
            ).wait_recv()
            for shift in range(1, halves):
                fold_side(j, shift).start()

        turn(1, slabs, piece)
        turn(0, slabs, lambda j: powers(half, j))
        power_copy(half).start()
        for shift in range(1, halves):
            part = lax.rem(half + halves - shift, halves)
            whole(fold_all.at[part], side_recv.at[shift - 1]).wait()
            turn(0, slabs, lambda j: powers(part, j))
            power_copy(part).start()
        whole(target_cot.at[1], side_sems.at[1]).wait()

        def cots(j, carry):
            for s in range(slices):
                z = j * slices + s
                total = -jnp.concatenate([target_cot[0, z], target_cot[1, z]], axis=0).astype(
                    jnp.float32
                )
                for other in range(total_slices):
                    total = total + gram_table[z, other : other + 1, :padded] * band_power[other]
                bc_send[j, s] = total.astype(jnp.bfloat16)
            return carry

        lax.fori_loop(0, slabs, cots, 0)
        turn(1, slabs, lambda step: bc_copy(step).start(), True)
        bc_own.start()
        part = jnp.zeros((solved, features), jnp.float32)
        for z in range(total_slices):
            j, s = divmod(z, slices)
            part = part + nn(bc_send[j, s], fold_all[s // own, j, s % own])
        oc_send[...] = (part * slope(pre_own[...])).astype(jnp.bfloat16)
        turn(1, slabs, lambda step: oc_copy(step).start(), True)
        oc_own.start()

    pl.when(solves)(solve)

    whole(cos_all.at[half], cos_sems.at[1]).wait()
    side_start(cos_all, cos_sems)
    forward(half)
    side_wait(cos_all, cos_sems)
    for shift in range(1, halves):
        forward(lax.rem(half + shift, halves))

    group_pairs = max(n for n in range(1, 9) if pairs % n == 0)

    def predict(i, carry):
        for n in range(group_pairs):
            p = i * group_pairs + n
            total = None
            for z in range(total_slices):
                term = pair_table[p, z : z + 1, :bands] * power_wide[z, :, :bands]
                total = term if total is None else total + term
            spectra_out[p] = total
        return carry

    mid_columns = mid_moment.shape[0]
    out_columns = out_moment.shape[0]
    pick_mid = onehot((mid_columns, width), me * mid_columns)
    pick_out = onehot((out_columns, features), me * out_columns)
    mid_own[...] = nt(pick_mid, trunk_mid[...])
    out_own[...] = nt(pick_out, trunk_out[...])
    in_own[...] = nt(trunk_in[...], pick_mid)
    mid_rows[...] = nn(pick_mid, trunk_mid[...]).astype(jnp.bfloat16)
    in_columns = nt(pick_mid, trunk_in[...]).astype(jnp.bfloat16)
    cosmology = cos_all[...].reshape(rows_all, params)
    in_slope[...] = slope(nt(in_columns, cosmology))
    cosmology_t[...] = nt(onehot((params, params), 0), cosmology).astype(jnp.bfloat16)
    mid_slope[...] = slope(pre_mid[...].reshape(rows_all, width))
    for i in (4, *range(10, 18)):
        loads[i].wait()

    pl.when(jnp.logical_not(solves))(whole(power_recv, side_sems.at[3]).wait)
    for z in range(total_slices):
        j, s = divmod(z, slices)
        power_wide[z] = power_recv[s // own, j * own + s % own].astype(jnp.float32)
    lax.fori_loop(0, pairs // group_pairs, predict, 0)
    whole(bc_recv.at[half], bc_sems.at[1]).wait()
    side_start(bc_recv, bc_sems)
    whole(oc_all.at[half], oc_sems.at[1]).wait()
    side_start(oc_all, oc_sems)
    side_wait(bc_recv, bc_sems)
    hidden_all = hidden[...].reshape(rows_all, features)
    for s in range(slices):
        cots = bc_recv[:, :, s].reshape(rows_all, padded)
        outer[s] = tn(hidden_all, cots).astype(jnp.bfloat16)
    early = pl.ds(0, early_new.shape[0])
    updated = adam_step(
        head_weight[0, early, :],
        head_moment[0, early, :],
        head_square[0, early, :],
        nn(outer[0, early, :], own_projection[0]),
    )
    for out, value in zip((early_new, early_moment, early_square), updated):
        out[...] = value
    side_wait(oc_all, oc_sems)
    oc_kept[...] = oc_all[...].reshape(rows_all, features)

    for shift in range(1, halves):
        for ref, sems in ((cos_all, cos_sems), (bc_recv, bc_sems), (oc_all, oc_sems)):
            whole(ref.at[half], sems.at[2]).wait()

    def sent_by_solver():
        whole(fold_all.at[half, pl.ds(0, solvers - 1)], fold_sems.at[0]).wait()
        for shift in range(1, halves):
            whole(fold_all.at[half], fold_sems.at[1]).wait()
        whole(bc_send.at[pl.ds(0, slabs - 1)], bc_sems.at[0]).wait()

        def step(i, carry):
            whole(oc_send, oc_sems.at[0]).wait()
            whole(cos_pair, cos_sems.at[0]).wait()
            return carry

        lax.fori_loop(0, slabs - 1, step, 0)
        whole(power_send, side_sems.at[2]).wait()

    def sent_by_other():
        whole(fold_all.at[half, pl.ds(0, solvers)], fold_sems.at[0]).wait()
        whole(target_cot.at[0], side_sems.at[0]).wait()
        whole(cos_pair.at[0], side_sems.at[4]).wait()

    pl.when(solves)(sent_by_solver)
    pl.when(jnp.logical_not(solves))(sent_by_other)


def update_kernel(slabs, halves, *refs):
    (
        spectra,
        outer,
        projection,
        head_weight,
        head_moment,
        head_square,
        in_moment,
        in_square,
        mid_moment,
        mid_square,
        out_moment,
        out_square,
        trunk_out,
        act_in,
        act_mid,
        oc_all,
        mid_slope,
        in_slope,
        mid_own,
        out_own,
        in_own,
        mid_rows,
        cosmology_t,
        *early,
    ) = refs[:26]
    results, made, store_sem, head_sem = refs[26:39], refs[39:51], refs[51], refs[52]
    head_out, trunk_made = made[:3], made[3:]
    me = lax.axis_index("gz") * halves + lax.axis_index("ba")
    slices, features, _ = head_weight.shape
    rows_all, _ = oc_all.shape
    width = mid_rows.shape[1]
    stores = [
        pltpu.make_async_copy(source, result, store_sem.at[i])
        for i, (source, result) in enumerate(zip((spectra, *trunk_made), (results[0], *results[4:])))
    ]
    first = early[0].shape[0]
    head_stores = [
        pltpu.make_async_copy(early[k], results[1 + k].at[0, pl.ds(0, first)], head_sem.at[k, 2 * slices])
        for k in range(3)
    ]
    for store in head_stores:
        store.start()
    stores[0].start()
    size = features // 2
    pieces = [
        (s, row) for s in range(slices) for row in range(0, features, size) if s or row >= first
    ]
    for n, (s, row) in enumerate(pieces):
        chunk = pl.ds(row, size)
        updated = adam_step(
            head_weight[s, chunk, :],
            head_moment[s, chunk, :],
            head_square[s, chunk, :],
            nn(outer[s, chunk, :], projection[s]),
        )
        for k, value in enumerate(updated):
            head_out[k][s, chunk, :] = value
            store = pltpu.make_async_copy(
                head_out[k].at[s, chunk], results[1 + k].at[s, chunk], head_sem.at[k, n]
            )
            store.start()
            head_stores.append(store)
    pick_mid = onehot((mid_moment.shape[0], width), me * mid_moment.shape[0])
    pick_out = onehot((out_moment.shape[0], oc_all.shape[1]), me * out_moment.shape[0])
    out_cot = oc_all[...]
    mid_cot = (nt(out_cot, trunk_out[...]) * mid_slope[...]).astype(jnp.bfloat16)
    out_cot_own = nt(pick_out, out_cot).astype(jnp.bfloat16)
    out_grad = nn(out_cot_own, act_mid[...].reshape(rows_all, width))
    mid_cot_own = nt(pick_mid, mid_cot).astype(jnp.bfloat16)
    mid_grad = nn(mid_cot_own, act_in[...].reshape(rows_all, width))
    in_cot_own = (nt(mid_rows[...], mid_cot) * in_slope[...]).astype(jnp.bfloat16)
    in_grad = nt(cosmology_t[...], in_cot_own)
    for first, own_weight, moment, square, gradient in (
        (0, mid_own, mid_moment, mid_square, mid_grad),
        (3, out_own, out_moment, out_square, out_grad),
        (6, in_own, in_moment, in_square, in_grad),
    ):
        updated = adam_step(own_weight[...], moment[...], square[...], gradient)
        for k, value in enumerate(updated):
            trunk_made[first + k][...] = value
            stores[1 + first + k].start()
    for store in (*stores, *head_stores):
        store.wait()


def shards(
    cosmology,
    trunk_in,
    trunk_mid,
    trunk_out,
    head_weight,
    band_width,
    band_weight,
    kernels,
    pair_bins,
    target,
    head_moment,
    head_square,
    in_moment,
    in_square,
    mid_moment,
    mid_square,
    out_moment,
    out_square,
):
    slabs = lax.axis_size("gz")
    halves = lax.axis_size("ba")
    count = slabs * halves
    rows, params = cosmology.shape
    pairs, bands = target.shape[1:]
    slices, features, cells = head_weight.shape
    width = trunk_mid.shape[0]
    rows_half = slabs * rows
    total_slices = slices * slabs
    own = slices // halves
    solvers = slabs // 2
    solved = 2 * rows
    padded = -(-bands // 8) * 8
    half_cells = cells // halves
    mid_columns = width // count
    out_columns = features // count
    bf16, f32 = jnp.bfloat16, jnp.float32
    hbm = pl.BlockSpec(memory_space=pltpu.HBM)
    vmem = pl.BlockSpec(memory_space=pltpu.VMEM)
    dma = pltpu.SemaphoreType.DMA
    inputs = (
        cosmology.T,
        trunk_in,
        trunk_mid,
        trunk_out,
        head_weight,
        band_width,
        band_weight,
        kernels,
        pair_bins.T,
        target.transpose(1, 0, 2),
        head_moment,
        head_square,
        in_moment,
        in_square,
        mid_moment.T,
        mid_square.T,
        out_moment.T,
        out_square.T,
    )
    inputs = tuple(pltpu.with_memory_space_constraint(a, pltpu.HBM) for a in inputs)
    out_shapes = [jax.ShapeDtypeStruct((pairs, rows, bands), f32)] + [
        jax.ShapeDtypeStruct(shape, dtype)
        for shape in (
            (slices, features, half_cells),
            (mid_columns, width),
            (out_columns, width),
            (params, mid_columns),
        )
        for dtype in (bf16, f32, f32)
    ]
    kept = [
        ((pairs, rows, bands), f32),
        ((slices, features, padded), bf16),
        ((slices, padded, half_cells), bf16),
        ((slices, features, half_cells), bf16),
        *((inputs[i].shape, inputs[i].dtype) for i in (*range(10, 18), 3)),
        ((halves, rows_half, width), bf16),
        ((halves, rows_half, width), bf16),
        ((halves * rows_half, features), bf16),
        ((halves * rows_half, width), f32),
        ((mid_columns, halves * rows_half), f32),
        ((mid_columns, width), f32),
        ((out_columns, width), f32),
        ((params, mid_columns), f32),
        ((mid_columns, width), bf16),
        ((params, halves * rows_half), bf16),
        *(((features // 2, half_cells), dtype) for dtype in (bf16, f32, f32)),
    ]
    kept = pl.pallas_call(
        functools.partial(step_kernel, slabs, halves, total_slices),
        out_shape=[pltpu.VMEM(*a) for a in kept],
        in_specs=[hbm] * len(inputs),
        out_specs=[vmem] * len(kept),
        scratch_shapes=[
            pltpu.VMEM(inputs[i].shape, inputs[i].dtype) for i in (0, 1, 2, 5, 6, 7, 8, 9)
        ]
        + [
            pltpu.VMEM((own, features, cells), bf16),
            pltpu.VMEM((halves, slabs, rows, params), bf16),
            pltpu.VMEM((2, rows, params), bf16),
            pltpu.VMEM((halves, rows_half, features), bf16),
            pltpu.VMEM((halves, rows_half, width), f32),
            pltpu.VMEM((solved, features), f32),
            pltpu.VMEM((slices, padded, cells), bf16),
            pltpu.VMEM((halves, slabs, own, padded, features), bf16),
            pltpu.VMEM((pairs, total_slices, lanes), f32),
            pltpu.VMEM((total_slices, total_slices, lanes), f32),
            pltpu.VMEM((2, total_slices, rows, padded), bf16),
            pltpu.VMEM((total_slices, solved, padded), f32),
            pltpu.VMEM((halves, slabs * own, rows, padded), bf16),
            pltpu.VMEM((halves, slabs * own, rows, padded), bf16),
            pltpu.VMEM((total_slices, rows, padded), f32),
            pltpu.VMEM((slabs, slices, solved, padded), bf16),
            pltpu.VMEM((halves, solvers, slices, solved, padded), bf16),
            pltpu.VMEM((solved, features), bf16),
            pltpu.VMEM((halves, solvers, solved, features), bf16),
            dma((len(inputs),)),
            dma,
            dma((2 + halves,)),
            dma((2,)),
            dma((slabs,)),
            dma((halves - 1,)),
            dma((6,)),
            dma((2 + halves,)),
            dma((2 + halves,)),
        ],
        compiler_params=pltpu.CompilerParams(
            collective_id=0, has_side_effects=True, vmem_limit_bytes=36 << 20
        ),
        name="step",
    )(*inputs)
    outs = pl.pallas_call(
        functools.partial(update_kernel, slabs, halves),
        out_shape=out_shapes,
        in_specs=[vmem] * len(kept),
        out_specs=[hbm] * len(out_shapes),
        scratch_shapes=[pltpu.VMEM(a.shape, a.dtype) for a in out_shapes[1:]]
        + [dma((len(out_shapes) - 3,)), dma((3, 2 * slices + 1))],
        compiler_params=pltpu.CompilerParams(vmem_limit_bytes=24 << 20),
        name="update",
    )(*kept)
    spectra, head, mid, out, inner = outs[0], outs[1:4], outs[4:7], outs[7:10], outs[10:13]
    return (
        spectra.transpose(1, 0, 2),
        *head,
        *inner,
        *(a.T for a in mid),
        *(a.T for a in out),
    )


def solution(mesh):
    placed = (
        P(("grp", "gz", "ba"), None),
        P(),
        P(),
        P(),
        P("gz", None, None),
        P("gz", None),
        P("gz", None),
        P(),
        P(),
        P(("grp", "gz", "ba"), None, None),
        P("gz", None, "ba"),
        P("gz", None, "ba"),
        P(None, ("gz", "ba")),
        P(None, ("gz", "ba")),
        P(None, ("gz", "ba")),
        P(None, ("gz", "ba")),
        P(None, ("gz", "ba")),
        P(None, ("gz", "ba")),
    )
    return jax.shard_map(
        shards,
        mesh=mesh,
        in_specs=placed,
        out_specs=(
            P(("grp", "gz", "ba"), None, None),
            P("gz", "grp", "ba"),
            P("gz", "grp", "ba"),
            P("gz", "grp", "ba"),
            P("grp", ("gz", "ba")),
            P("grp", ("gz", "ba")),
            P("grp", ("gz", "ba")),
            P("grp", ("gz", "ba")),
            P("grp", ("gz", "ba")),
            P("grp", ("gz", "ba")),
            P("grp", ("gz", "ba")),
            P("grp", ("gz", "ba")),
            P("grp", ("gz", "ba")),
        ),
        check_vma=False,
    )
```

```python
import functools
import math

import jax
import jax.numpy as jnp
from jax import lax
from jax.experimental import pallas as pl
from jax.experimental.pallas import tpu as pltpu
from jax.sharding import PartitionSpec as P

learn_rate = 0.001
beta_first = 0.9
beta_second = 0.999
adam_epsilon = 1e-08
lanes = 128
MESH = pl.DeviceIdType.MESH
highest = lax.Precision.HIGHEST


def adam_step(weight, moment, square, gradient):
    moment_new = beta_first * moment + (1.0 - beta_first) * gradient
    square_new = beta_second * square + (1.0 - beta_second) * gradient * gradient
    updated = weight.astype(jnp.float32) - learn_rate * moment_new / (
        jnp.sqrt(square_new) + adam_epsilon
    )
    return (updated.astype(jnp.bfloat16), moment_new, square_new)


def nn(a, b, precision=None):
    return lax.dot_general(
        a, b, (((1,), (0,)), ((), ())), preferred_element_type=jnp.float32, precision=precision
    )


def nt(a, b, precision=None):
    return lax.dot_general(
        a, b, (((1,), (1,)), ((), ())), preferred_element_type=jnp.float32, precision=precision
    )


def tn(a, b, precision=None):
    return lax.dot_general(
        a, b, (((0,), (0,)), ((), ())), preferred_element_type=jnp.float32, precision=precision
    )


def split(values):
    high = values.astype(jnp.bfloat16)
    low = (values - high.astype(jnp.float32)).astype(jnp.bfloat16)
    return high, low


def iota(shape, axis):
    return lax.broadcasted_iota(jnp.int32, shape, axis)


def onehot(shape, offset, dtype=jnp.bfloat16):
    return (iota(shape, 0) + offset == iota(shape, 1)).astype(dtype)


def quotient(values, by):
    if by & (by - 1) == 0:
        return values >> (by.bit_length() - 1)
    return values // by


def remainder(values, by):
    if by & (by - 1) == 0:
        return values & (by - 1)
    return values % by


def step_kernel(slabs, halves, total_slices, *refs):
    inputs, refs = refs[:18], refs[18:]
    (
        spectra_out,
        outer,
        own_projection,
        head_weight,
        head_moment,
        head_square,
        in_moment,
        in_square,
        mid_moment,
        mid_square,
        out_moment,
        out_square,
        trunk_out,
        act_in,
        act_mid,
        oc_kept,
        mid_slope,
        in_slope,
        mid_own,
        out_own,
        in_own,
        mid_rows,
        cosmology_t,
        early_new,
        early_moment,
        early_square,
        cos_t,
        trunk_in,
        trunk_mid,
        band_width,
        band_weight,
        kernels,
        pair_bins,
        target,
        fold_weight,
        cos_all,
        cos_pair,
        hidden,
        pre_mid,
        pre_own,
        projection,
        fold_all,
        pair_table,
        gram_table,
        target_cot,
        band_power,
        band_cot,
        power_send,
        power_recv,
        power_wide,
        bc_send,
        bc_recv,
        oc_send,
        oc_all,
        load_sem,
        fold_load,
        cos_sems,
        fold_sems,
        fold_recv,
        side_recv,
        side_sems,
        bc_sems,
        oc_sems,
    ) = refs
    held = (
        cos_t,
        trunk_in,
        trunk_mid,
        trunk_out,
        head_weight,
        band_width,
        band_weight,
        kernels,
        pair_bins,
        target,
        head_moment,
        head_square,
        in_moment,
        in_square,
        mid_moment,
        mid_square,
        out_moment,
        out_square,
    )
    group = lax.axis_index("grp")
    slab = lax.axis_index("gz")
    half = lax.axis_index("ba")
    count = slabs * halves
    me = slab * halves + half
    params, rows = cos_t.shape
    pairs, _, bands = target.shape
    slices, features, half_cells = head_weight.shape
    own = slices // halves
    cells = fold_weight.shape[2]
    padded = projection.shape[1]
    width = trunk_mid.shape[0]
    rows_half = slabs * rows
    rows_all = halves * rows_half
    solvers = slabs // 2
    quarter = slabs // 4
    solved = 2 * rows

    solves = (slab >= quarter) & (slab < quarter + solvers)
    below = slab < quarter
    solver = jnp.where(below, slab, jnp.where(solves, slab - quarter, slab - solvers))
    solver_slab = solver + quarter
    outer_slab = jnp.where(solver < quarter, solver, solver + solvers)

    def exclusive(a, b):
        return a + b - 2 * (a & b)

    def slab_at(step):
        near = exclusive(solver, quotient(step, 2))
        far = jnp.where(near < quarter, near, near + solvers)
        if isinstance(step, int):
            return far if step % 2 else near + quarter
        return jnp.where(remainder(step, 2) == 1, far, near + quarter)

    def turn(first, last, body, backward=False):
        if last - first <= 16:
            for d in range(first, last):
                body(first + last - 1 - d if backward else d)
        else:

            def step(d, carry):
                body(first + last - 1 - d if backward else d)
                return carry

            lax.fori_loop(first, last, step, 0)

    start = pl.multiple_of(half * half_cells, half_cells)
    own_cells = pl.ds(start, half_cells)
    own_slices = pl.ds(half * own, own)
    loads = [
        pltpu.make_async_copy(
            source.at[:, :, own_cells] if i == 4 else source, kept, load_sem.at[i]
        )
        for i, (source, kept) in enumerate(zip(inputs, held))
    ]
    fold_copy = pltpu.make_async_copy(inputs[4].at[own_slices], fold_weight, fold_load)
    for i in (5, 6):
        loads[i].start()
    fold_copy.start()
    for i in (0, 7, 8, 1, 2, 3, 9):
        loads[i].start()

    barrier = pltpu.get_barrier_semaphore()

    def greet(step):
        pl.semaphore_signal(
            barrier, inc=1, device_id=(group, slab_at(step), half), device_id_type=MESH
        )

    def side(shift):
        return (group, slab, lax.rem(half + shift, halves))

    pl.when(solves)(lambda: turn(1, slabs, greet, True))
    pl.when(jnp.logical_not(solves))(
        lambda: turn(0, solvers, lambda step: greet(2 * step), True)
    )
    for shift in range(1, halves):
        pl.semaphore_signal(barrier, inc=1, device_id=side(shift), device_id_type=MESH)

    loads[5].wait()
    loads[6].wait()
    triangle = iota((padded, bands), 0)
    column = iota((padded, bands), 1)
    widths = band_width[...].astype(jnp.float32).astype(jnp.bfloat16)
    ends = nt((triangle >= column).astype(jnp.bfloat16), widths).astype(jnp.int32)
    starts = nt((triangle > column).astype(jnp.bfloat16), widths).astype(jnp.int32)
    cell = iota((padded, cells), 1)
    for s in range(slices):
        member = (starts[:, s : s + 1] <= cell) & (cell < ends[:, s : s + 1])
        weighted = jnp.where(member, band_weight[s : s + 1, :], 0.0)
        total = jnp.maximum(jnp.sum(weighted, axis=1, keepdims=True), 1e-30)
        projection[s] = (weighted * (1.0 / total)).astype(jnp.bfloat16)
    fold_copy.wait()
    for k in range(own):
        fold = nt(projection[half * own + k], fold_weight[k])
        fold_all[half, slab, k] = fold.astype(jnp.bfloat16)
    loads[0].wait()
    cos_own = nt(onehot((rows, rows), 0), cos_t[...]).astype(jnp.bfloat16)
    cos_pair[0] = cos_own
    pl.semaphore_wait(barrier, jnp.where(solves, slabs - 1, solvers) + halves - 1)

    def cos_copy(step):
        return pltpu.make_async_remote_copy(
            src_ref=cos_pair,
            dst_ref=cos_all.at[half, pl.ds(2 * solver, 2)],
            send_sem=cos_sems.at[0],
            recv_sem=cos_sems.at[1],
            device_id=(group, slab_at(step), half),
            device_id_type=MESH,
        )

    def fold_send(step):
        return pltpu.make_async_remote_copy(
            src_ref=fold_all.at[half, slab],
            dst_ref=fold_all.at[half, slab],
            send_sem=fold_sems.at[0],
            recv_sem=fold_recv.at[slab],
            device_id=(group, exclusive(solver, step) + quarter, half),
            device_id_type=MESH,
        )

    cos_near = pltpu.make_async_remote_copy(
        src_ref=cos_pair.at[0],
        dst_ref=cos_pair.at[1],
        send_sem=side_sems.at[4],
        recv_sem=side_sems.at[5],
        device_id=(group, solver_slab, half),
        device_id_type=MESH,
    )
    pl.when(jnp.logical_not(solves))(cos_near.start)
    turn(1, solvers, lambda step: fold_send(step).start(), True)
    pl.when(jnp.logical_not(solves))(lambda: fold_send(0).start())
    for i in range(10, 18):
        loads[i].start()
    loads[4].start()

    for i in (7, 8):
        loads[i].wait()
    bins = kernels.shape[0]
    weights = 8.0 / math.sqrt(total_slices)
    for piece in range(2):
        chosen = (iota((bins, pairs), 0) == pair_bins[piece : piece + 1, :]).astype(jnp.float32)
        weights = weights * tn(kernels[...], chosen, highest)
    for p in range(pairs):
        pair_table[p] = jnp.broadcast_to(weights[:, p : p + 1], (total_slices, lanes))
    loads[9].wait()
    target_cot[0] = jnp.zeros_like(target_cot[0])
    block = math.gcd(total_slices, 16)
    for first in range(0, total_slices, block):

        def gather(p, sums):
            values = target[p]
            return tuple(
                old + pair_table[p, first + z : first + z + 1, :bands] * values
                for z, old in enumerate(sums)
            )

        sums = lax.fori_loop(
            0, pairs, gather, tuple(jnp.zeros((rows, bands), jnp.float32) for _ in range(block))
        )
        for z, values in enumerate(sums):
            target_cot[0, first + z, :, :bands] = values.astype(jnp.bfloat16)

    target_copy = pltpu.make_async_remote_copy(
        src_ref=target_cot.at[0],
        dst_ref=target_cot.at[1],
        send_sem=side_sems.at[0],
        recv_sem=side_sems.at[1],
        device_id=(group, solver_slab, half),
        device_id_type=MESH,
    )
    pl.when(jnp.logical_not(solves))(target_copy.start)
    for s in range(slices):
        own_projection[s] = projection[s, :, own_cells]

    for i in (1, 2, 3):
        loads[i].wait()

    def whole(ref, semaphore):
        return pltpu.make_async_copy(ref, ref, semaphore)

    def forward(part):
        cosmology = cos_all[part].reshape(rows_half, params)
        pre = nn(cosmology, trunk_in[...])
        act = (pre * jax.nn.sigmoid(pre)).astype(jnp.bfloat16)
        act_in[part] = act
        pre = nn(act, trunk_mid[...])
        pre_mid[part] = pre
        act = (pre * jax.nn.sigmoid(pre)).astype(jnp.bfloat16)
        act_mid[part] = act
        pre = nn(act, trunk_out[...])
        act = (pre * jax.nn.sigmoid(pre)).astype(jnp.bfloat16)
        hidden[part] = act

    def slope(values):
        sigmoid = jax.nn.sigmoid(values)
        return sigmoid * (1.0 + values * (1.0 - sigmoid))

    def side_copy(ref, sems, shift):
        return pltpu.make_async_remote_copy(
            src_ref=ref.at[half],
            dst_ref=ref.at[half],
            send_sem=sems.at[2],
            recv_sem=sems.at[2 + shift],
            device_id=side(shift),
            device_id_type=MESH,
        )

    def side_start(ref, sems):
        for shift in range(1, halves):
            side_copy(ref, sems, shift).start()

    def side_wait(ref, sems):
        for shift in range(1, halves):
            whole(ref.at[lax.rem(half + halves - shift, halves)], sems.at[2 + shift]).wait()


    def fold_side(j, shift):
        return pltpu.make_async_remote_copy(
            src_ref=fold_all.at[half, j],
            dst_ref=fold_all.at[half, j],
            send_sem=fold_sems.at[1],
            recv_sem=side_recv.at[shift - 1],
            device_id=side(shift),
            device_id_type=MESH,
        )

    def bc_copy(step):
        return pltpu.make_async_remote_copy(
            src_ref=bc_send.at[slab_at(step)],
            dst_ref=bc_recv.at[half, solver],
            send_sem=bc_sems.at[0],
            recv_sem=bc_sems.at[1],
            device_id=(group, slab_at(step), half),
            device_id_type=MESH,
        )

    def oc_copy(step):
        return pltpu.make_async_remote_copy(
            src_ref=oc_send,
            dst_ref=oc_all.at[half, solver],
            send_sem=oc_sems.at[0],
            recv_sem=oc_sems.at[1],
            device_id=(group, slab_at(step), half),
            device_id_type=MESH,
        )

    def power_copy(part):
        return pltpu.make_async_remote_copy(
            src_ref=power_send.at[part],
            dst_ref=power_recv.at[part],
            send_sem=side_sems.at[2],
            recv_sem=side_sems.at[3],
            device_id=(group, outer_slab, half),
            device_id_type=MESH,
        )

    bc_own = pltpu.make_async_copy(bc_send.at[slab], bc_recv.at[half, solver], bc_sems.at[1])
    oc_own = pltpu.make_async_copy(oc_send, oc_all.at[half, solver], oc_sems.at[1])

    def solve():
        for shift in range(1, halves):
            fold_side(slab, shift).start()
        whole(cos_pair.at[1], side_sems.at[5]).wait()
        turn(1, slabs, lambda step: cos_copy(step).start(), True)
        pltpu.make_async_copy(
            cos_pair, cos_all.at[half, pl.ds(2 * solver, 2)], cos_sems.at[1]
        ).start()
        act = cos_pair[...].reshape(solved, params)
        for layer in (trunk_in, trunk_mid, trunk_out):
            pre = nn(act, layer[...])
            act = (pre * jax.nn.sigmoid(pre)).astype(jnp.bfloat16)
        pre_own[...] = pre
        features_own = act

        def powers(part, j):
            for k in range(own):
                z = (j * halves + part) * own + k
                power = nt(features_own, fold_all[part, j, k])
                band_power[z] = power
                power = power.astype(jnp.bfloat16)
                power_recv[part, j * own + k] = power[:rows]
                power_send[part, j * own + k] = power[rows:]

        for z in range(total_slices):
            both = jnp.sum(weights * weights[z : z + 1, :], axis=1, keepdims=True)
            gram_table[z] = jnp.broadcast_to(both, (total_slices, lanes))

        def piece(step):
            j = slab_at(step)
            pltpu.make_async_remote_copy(
                src_ref=fold_all.at[half, j],
                dst_ref=fold_all.at[half, j],
                send_sem=fold_sems.at[0],
                recv_sem=fold_recv.at[j],
                device_id=(group, j, half),
                device_id_type=MESH,
            ).wait_recv()
            for shift in range(1, halves):
                fold_side(j, shift).start()

        turn(1, slabs, piece)
        turn(0, slabs, lambda j: powers(half, j))
        power_copy(half).start()
        for shift in range(1, halves):
            part = lax.rem(half + halves - shift, halves)
            whole(fold_all.at[part], side_recv.at[shift - 1]).wait()
            turn(0, slabs, lambda j: powers(part, j))
            power_copy(part).start()

        def cots(j, carry):
            for s in range(slices):
                z = j * slices + s
                total = gram_table[z, 0:1, :padded] * band_power[0]
                for other in range(1, total_slices):
                    total = total + gram_table[z, other : other + 1, :padded] * band_power[other]
                band_cot[z] = total
            return carry

        lax.fori_loop(0, slabs, cots, 0)
        slope_own = slope(pre_own[...])
        whole(target_cot.at[1], side_sems.at[1]).wait()
        for z in range(total_slices):
            shift_cot = jnp.concatenate([target_cot[0, z], target_cot[1, z]], axis=0)
            total = band_cot[z] - shift_cot.astype(jnp.float32)
            bc_send[z // slices, z % slices] = total.astype(jnp.bfloat16)
        turn(1, slabs, lambda step: bc_copy(step).start(), True)
        bc_own.start()
        part = jnp.zeros((solved, features), jnp.float32)
        for z in range(total_slices):
            j, s = divmod(z, slices)
            part = part + nn(bc_send[j, s], fold_all[s // own, j, s % own])
        oc_send[...] = (part * slope_own).astype(jnp.bfloat16)
        turn(1, slabs, lambda step: oc_copy(step).start(), True)
        oc_own.start()

    pl.when(solves)(solve)

    whole(cos_all.at[half], cos_sems.at[1]).wait()
    side_start(cos_all, cos_sems)
    forward(half)
    side_wait(cos_all, cos_sems)
    for shift in range(1, halves):
        forward(lax.rem(half + shift, halves))

    group_pairs = max(n for n in range(1, 9) if pairs % n == 0)

    def predict(i, carry):
        for n in range(group_pairs):
            p = i * group_pairs + n
            total = None
            for z in range(total_slices):
                term = pair_table[p, z : z + 1, :bands] * power_wide[z, :, :bands]
                total = term if total is None else total + term
            spectra_out[p] = total
        return carry

    mid_columns = mid_moment.shape[0]
    out_columns = out_moment.shape[0]
    pick_mid = onehot((mid_columns, width), me * mid_columns)
    pick_out = onehot((out_columns, features), me * out_columns)
    mid_own[...] = nt(pick_mid, trunk_mid[...])
    out_own[...] = nt(pick_out, trunk_out[...])
    in_own[...] = nt(trunk_in[...], pick_mid)
    mid_rows[...] = nn(pick_mid, trunk_mid[...]).astype(jnp.bfloat16)
    in_columns = nt(pick_mid, trunk_in[...]).astype(jnp.bfloat16)
    cosmology = cos_all[...].reshape(rows_all, params)
    in_slope[...] = slope(nt(in_columns, cosmology))
    cosmology_t[...] = nt(onehot((params, params), 0), cosmology).astype(jnp.bfloat16)
    mid_slope[...] = slope(pre_mid[...].reshape(rows_all, width))
    for i in (4, *range(10, 18)):
        loads[i].wait()

    pl.when(jnp.logical_not(solves))(whole(power_recv, side_sems.at[3]).wait)
    for z in range(total_slices):
        j, s = divmod(z, slices)
        power_wide[z] = power_recv[s // own, j * own + s % own].astype(jnp.float32)
    lax.fori_loop(0, pairs // group_pairs, predict, 0)
    whole(bc_recv.at[half], bc_sems.at[1]).wait()
    side_start(bc_recv, bc_sems)
    whole(oc_all.at[half], oc_sems.at[1]).wait()
    side_start(oc_all, oc_sems)
    side_wait(bc_recv, bc_sems)
    hidden_all = hidden[...].reshape(rows_all, features)
    for s in range(slices):
        cots = bc_recv[:, :, s].reshape(rows_all, padded)
        outer[s] = tn(hidden_all, cots).astype(jnp.bfloat16)
    early = pl.ds(0, early_new.shape[0])
    updated = adam_step(
        head_weight[0, early, :],
        head_moment[0, early, :],
        head_square[0, early, :],
        nn(outer[0, early, :], own_projection[0]),
    )
    for out, value in zip((early_new, early_moment, early_square), updated):
        out[...] = value
    side_wait(oc_all, oc_sems)
    oc_kept[...] = oc_all[...].reshape(rows_all, features)

    for shift in range(1, halves):
        for ref, sems in ((cos_all, cos_sems), (bc_recv, bc_sems), (oc_all, oc_sems)):
            whole(ref.at[half], sems.at[2]).wait()

    def sent_by_solver():
        whole(fold_all.at[half, pl.ds(0, solvers - 1)], fold_sems.at[0]).wait()
        for shift in range(1, halves):
            whole(fold_all.at[half], fold_sems.at[1]).wait()
        whole(bc_send.at[pl.ds(0, slabs - 1)], bc_sems.at[0]).wait()

        def step(i, carry):
            whole(oc_send, oc_sems.at[0]).wait()
            whole(cos_pair, cos_sems.at[0]).wait()
            return carry

        lax.fori_loop(0, slabs - 1, step, 0)
        whole(power_send, side_sems.at[2]).wait()

    def sent_by_other():
        whole(fold_all.at[half, pl.ds(0, solvers)], fold_sems.at[0]).wait()
        whole(target_cot.at[0], side_sems.at[0]).wait()
        whole(cos_pair.at[0], side_sems.at[4]).wait()

    pl.when(solves)(sent_by_solver)
    pl.when(jnp.logical_not(solves))(sent_by_other)


def update_kernel(slabs, halves, *refs):
    (
        spectra,
        outer,
        projection,
        head_weight,
        head_moment,
        head_square,
        in_moment,
        in_square,
        mid_moment,
        mid_square,
        out_moment,
        out_square,
        trunk_out,
        act_in,
        act_mid,
        oc_all,
        mid_slope,
        in_slope,
        mid_own,
        out_own,
        in_own,
        mid_rows,
        cosmology_t,
        *early,
    ) = refs[:26]
    results, made, store_sem, head_sem = refs[26:39], refs[39:51], refs[51], refs[52]
    head_out, trunk_made = made[:3], made[3:]
    me = lax.axis_index("gz") * halves + lax.axis_index("ba")
    slices, features, _ = head_weight.shape
    rows_all, _ = oc_all.shape
    width = mid_rows.shape[1]
    stores = [
        pltpu.make_async_copy(source, result, store_sem.at[i])
        for i, (source, result) in enumerate(zip((spectra, *trunk_made), (results[0], *results[4:])))
    ]
    first = early[0].shape[0]
    head_stores = [
        pltpu.make_async_copy(early[k], results[1 + k].at[0, pl.ds(0, first)], head_sem.at[k, 2 * slices])
        for k in range(3)
    ]
    for store in head_stores:
        store.start()
    stores[0].start()
    size = features // 2
    pieces = [
        (s, row) for s in range(slices) for row in range(0, features, size) if s or row >= first
    ]
    for n, (s, row) in enumerate(pieces):
        chunk = pl.ds(row, size)
        updated = adam_step(
            head_weight[s, chunk, :],
            head_moment[s, chunk, :],
            head_square[s, chunk, :],
            nn(outer[s, chunk, :], projection[s]),
        )
        for k, value in enumerate(updated):
            head_out[k][s, chunk, :] = value
            store = pltpu.make_async_copy(
                head_out[k].at[s, chunk], results[1 + k].at[s, chunk], head_sem.at[k, n]
            )
            store.start()
            head_stores.append(store)
    pick_mid = onehot((mid_moment.shape[0], width), me * mid_moment.shape[0])
    pick_out = onehot((out_moment.shape[0], oc_all.shape[1]), me * out_moment.shape[0])
    out_cot = oc_all[...]
    mid_cot = (nt(out_cot, trunk_out[...]) * mid_slope[...]).astype(jnp.bfloat16)
    out_cot_own = nt(pick_out, out_cot).astype(jnp.bfloat16)
    out_grad = nn(out_cot_own, act_mid[...].reshape(rows_all, width))
    mid_cot_own = nt(pick_mid, mid_cot).astype(jnp.bfloat16)
    mid_grad = nn(mid_cot_own, act_in[...].reshape(rows_all, width))
    in_cot_own = (nt(mid_rows[...], mid_cot) * in_slope[...]).astype(jnp.bfloat16)
    in_grad = nt(cosmology_t[...], in_cot_own)
    for first, own_weight, moment, square, gradient in (
        (0, mid_own, mid_moment, mid_square, mid_grad),
        (3, out_own, out_moment, out_square, out_grad),
        (6, in_own, in_moment, in_square, in_grad),
    ):
        updated = adam_step(own_weight[...], moment[...], square[...], gradient)
        for k, value in enumerate(updated):
            trunk_made[first + k][...] = value
            stores[1 + first + k].start()
    for store in (*stores, *head_stores):
        store.wait()


def shards(
    cosmology,
    trunk_in,
    trunk_mid,
    trunk_out,
    head_weight,
    band_width,
    band_weight,
    kernels,
    pair_bins,
    target,
    head_moment,
    head_square,
    in_moment,
    in_square,
    mid_moment,
    mid_square,
    out_moment,
    out_square,
):
    slabs = lax.axis_size("gz")
    halves = lax.axis_size("ba")
    count = slabs * halves
    rows, params = cosmology.shape
    pairs, bands = target.shape[1:]
    slices, features, cells = head_weight.shape
    width = trunk_mid.shape[0]
    rows_half = slabs * rows
    total_slices = slices * slabs
    own = slices // halves
    solvers = slabs // 2
    solved = 2 * rows
    padded = -(-bands // 8) * 8
    half_cells = cells // halves
    mid_columns = width // count
    out_columns = features // count
    bf16, f32 = jnp.bfloat16, jnp.float32
    hbm = pl.BlockSpec(memory_space=pltpu.HBM)
    vmem = pl.BlockSpec(memory_space=pltpu.VMEM)
    dma = pltpu.SemaphoreType.DMA
    inputs = (
        cosmology.T,
        trunk_in,
        trunk_mid,
        trunk_out,
        head_weight,
        band_width,
        band_weight,
        kernels,
        pair_bins.T,
        target.transpose(1, 0, 2),
        head_moment,
        head_square,
        in_moment,
        in_square,
        mid_moment.T,
        mid_square.T,
        out_moment.T,
        out_square.T,
    )
    inputs = tuple(pltpu.with_memory_space_constraint(a, pltpu.HBM) for a in inputs)
    out_shapes = [jax.ShapeDtypeStruct((pairs, rows, bands), f32)] + [
        jax.ShapeDtypeStruct(shape, dtype)
        for shape in (
            (slices, features, half_cells),
            (mid_columns, width),
            (out_columns, width),
            (params, mid_columns),
        )
        for dtype in (bf16, f32, f32)
    ]
    kept = [
        ((pairs, rows, bands), f32),
        ((slices, features, padded), bf16),
        ((slices, padded, half_cells), bf16),
        ((slices, features, half_cells), bf16),
        *((inputs[i].shape, inputs[i].dtype) for i in (*range(10, 18), 3)),
        ((halves, rows_half, width), bf16),
        ((halves, rows_half, width), bf16),
        ((halves * rows_half, features), bf16),
        ((halves * rows_half, width), f32),
        ((mid_columns, halves * rows_half), f32),
        ((mid_columns, width), f32),
        ((out_columns, width), f32),
        ((params, mid_columns), f32),
        ((mid_columns, width), bf16),
        ((params, halves * rows_half), bf16),
        *(((features // 2, half_cells), dtype) for dtype in (bf16, f32, f32)),
    ]
    kept = pl.pallas_call(
        functools.partial(step_kernel, slabs, halves, total_slices),
        out_shape=[pltpu.VMEM(*a) for a in kept],
        in_specs=[hbm] * len(inputs),
        out_specs=[vmem] * len(kept),
        scratch_shapes=[
            pltpu.VMEM(inputs[i].shape, inputs[i].dtype) for i in (0, 1, 2, 5, 6, 7, 8, 9)
        ]
        + [
            pltpu.VMEM((own, features, cells), bf16),
            pltpu.VMEM((halves, slabs, rows, params), bf16),
            pltpu.VMEM((2, rows, params), bf16),
            pltpu.VMEM((halves, rows_half, features), bf16),
            pltpu.VMEM((halves, rows_half, width), f32),
            pltpu.VMEM((solved, features), f32),
            pltpu.VMEM((slices, padded, cells), bf16),
            pltpu.VMEM((halves, slabs, own, padded, features), bf16),
            pltpu.VMEM((pairs, total_slices, lanes), f32),
            pltpu.VMEM((total_slices, total_slices, lanes), f32),
            pltpu.VMEM((2, total_slices, rows, padded), bf16),
            pltpu.VMEM((total_slices, solved, padded), f32),
            pltpu.VMEM((total_slices, solved, padded), f32),
            pltpu.VMEM((halves, slabs * own, rows, padded), bf16),
            pltpu.VMEM((halves, slabs * own, rows, padded), bf16),
            pltpu.VMEM((total_slices, rows, padded), f32),
            pltpu.VMEM((slabs, slices, solved, padded), bf16),
            pltpu.VMEM((halves, solvers, slices, solved, padded), bf16),
            pltpu.VMEM((solved, features), bf16),
            pltpu.VMEM((halves, solvers, solved, features), bf16),
            dma((len(inputs),)),
            dma,
            dma((2 + halves,)),
            dma((2,)),
            dma((slabs,)),
            dma((halves - 1,)),
            dma((6,)),
            dma((2 + halves,)),
            dma((2 + halves,)),
        ],
        compiler_params=pltpu.CompilerParams(
            collective_id=0, has_side_effects=True, vmem_limit_bytes=36 << 20
        ),
        name="step",
    )(*inputs)
    outs = pl.pallas_call(
        functools.partial(update_kernel, slabs, halves),
        out_shape=out_shapes,
        in_specs=[vmem] * len(kept),
        out_specs=[hbm] * len(out_shapes),
        scratch_shapes=[pltpu.VMEM(a.shape, a.dtype) for a in out_shapes[1:]]
        + [dma((len(out_shapes) - 3,)), dma((3, 2 * slices + 1))],
        compiler_params=pltpu.CompilerParams(vmem_limit_bytes=24 << 20),
        name="update",
    )(*kept)
    spectra, head, mid, out, inner = outs[0], outs[1:4], outs[4:7], outs[7:10], outs[10:13]
    return (
        spectra.transpose(1, 0, 2),
        *head,
        *inner,
        *(a.T for a in mid),
        *(a.T for a in out),
    )


def solution(mesh):
    placed = (
        P(("grp", "gz", "ba"), None),
        P(),
        P(),
        P(),
        P("gz", None, None),
        P("gz", None),
        P("gz", None),
        P(),
        P(),
        P(("grp", "gz", "ba"), None, None),
        P("gz", None, "ba"),
        P("gz", None, "ba"),
        P(None, ("gz", "ba")),
        P(None, ("gz", "ba")),
        P(None, ("gz", "ba")),
        P(None, ("gz", "ba")),
        P(None, ("gz", "ba")),
        P(None, ("gz", "ba")),
    )
    return jax.shard_map(
        shards,
        mesh=mesh,
        in_specs=placed,
        out_specs=(
            P(("grp", "gz", "ba"), None, None),
            P("gz", "grp", "ba"),
            P("gz", "grp", "ba"),
            P("gz", "grp", "ba"),
            P("grp", ("gz", "ba")),
            P("grp", ("gz", "ba")),
            P("grp", ("gz", "ba")),
            P("grp", ("gz", "ba")),
            P("grp", ("gz", "ba")),
            P("grp", ("gz", "ba")),
            P("grp", ("gz", "ba")),
            P("grp", ("gz", "ba")),
            P("grp", ("gz", "ba")),
        ),
        check_vma=False,
    )
```
